768 devices in a mesh: gx: 96 (over y_lo, z, core), gy: 8 (over x, y_hi).
Axes of the slice: x: 4, y: 8 (y_hi: 2, y_lo: 4; y = y_hi * 4 + y_lo), z: 12, core: 2. Of those that a mesh axis runs over, the one named last changes fastest.
Arguments:
- position: float32 [3, 192, 32, 128], P(None, 'gx', 'gy'), may hold values from 0 to 48, as said below
- velocity: float32 [3, 192, 32, 128], P(None, 'gx', 'gy'), may hold values from -12 to 12
- force_old: float32 [3, 192, 32, 128], P(None, 'gx', 'gy'), may hold values from -6 to 6
- counts: int32 [192, 32], P('gx', 'gy'), may hold values from 64 to 128
- density_coef: float32 [4], replicated, may hold values from 0.02 to 0.08
- pair_coef: float32 [4], replicated, may hold values from 0.5 to 2.5
- embed_coef: float32 [2], replicated, may hold values from 0.2 to 2
Outputs:
- position_new: float32 [3, 192, 32, 128], P(None, 'gx', 'gy')
- velocity_new: float32 [3, 192, 32, 128], P(None, 'gx', 'gy')
- force_new: float32 [3, 192, 32, 128], P(None, 'gx', 'gy')
- stress: float32 [6, 192, 32, 128], P(None, 'gx', 'gy')
The draws below stay inside these ranges and needn't reach their ends.
Inputs may be any that keep to these rules, and one draw needn't show every extreme that they name: A block's live atoms occupy its first counts slots. `position`: coordinates stay within a margin of the atom's own cell block column.
All inputs are finite; a program needn't handle non-finite values.
Results may differ from the reference program's by a relative error of at most 0.0003.
Values sent between devices are 32-bit elements; how exact they have to be, the bound alone decides.
No kernel may reach another device: no remote copies, remote signals or barrier semaphores. Data moves between devices by JAX's collectives and lax.ppermute only.
A program may use at most 32 MiB of HBM per device.

```python
import math
import jax
import jax.numpy as jnp
from jax import lax

ATOMS = 128
NBX = 192
NBY = 32


def draw_position(key, part):
    slot_index = jnp.arange(ATOMS, dtype=jnp.int32)
    layers = slot_index // 4
    stagger = 0.5 * (layers % 2).astype(jnp.float32) + 0.25
    across = (slot_index % 4 // 2).astype(jnp.float32) + stagger
    second = (slot_index % 2).astype(jnp.float32) + stagger
    height = (layers.astype(jnp.float32) + 0.5) * 1.5
    lattice = jnp.stack([across * 2.75, second * 2.75, height])
    full_shape = (3, NBX, NBY, ATOMS)
    order_key = jax.random.fold_in(key, 17)
    jitter_key = jax.random.fold_in(key, 29)
    scores = jax.random.randint(order_key, (NBX, NBY, ATOMS), 0, 1048576, dtype=jnp.int32) * ATOMS + slot_index
    order = jnp.argsort(scores, axis=2)
    placed = jnp.take(lattice, order, axis=1)
    jitter = jnp.clip(0.25 * jax.random.normal(jitter_key, full_shape, jnp.float32), -0.6, 0.6)
    return placed + jitter


def plant(values, rng, smallest, top_value):
    index_at = [jax.random.randint(jax.random.fold_in(rng, axis), (), 0, length) for axis, length in enumerate(values.shape)]
    widest = values.shape.index(max(values.shape))
    neighbour = index_at[:widest] + [(index_at[widest] + 1) % values.shape[widest]] + index_at[widest + 1:]
    return values.at[tuple(index_at)].set(smallest).at[tuple(neighbour)].set(top_value)


def steps_of(own_key, shape, cuts, smallest, top_value):
    loudness = 1.0
    for axis_at, parts in cuts:
        steps = jax.random.uniform(jax.random.fold_in(jax.random.fold_in(own_key, 6), axis_at), (parts,), jnp.float32, smallest / len(cuts), top_value / len(cuts))
        loudness = loudness * jnp.repeat(jnp.exp(steps), shape[axis_at] // parts).reshape((-1,) + (1,) * (len(shape) - 1 - axis_at))
    return loudness


def scatter_about(own_key, dims, width, bound, cuts=(), kind=jnp.bfloat16):
    gain = steps_of(own_key, dims, cuts, -0.22, 0.18) if cuts else 1.0
    values = jax.random.normal(own_key, dims, jnp.float32) * width * gain
    return jnp.minimum(jnp.maximum(values, -bound), bound).astype(kind)


def setup_inputs(seed: int = 0) -> dict:
    key_of = jax.random.split(jax.random.key(seed), 8)
    return {
        "position": draw_position(jax.random.fold_in(key_of[7], 71), 0),
        "velocity": scatter_about(key_of[1], (3, NBX, NBY, ATOMS), 2.0, 12.0, ((1, 96), (2, 8)), jnp.float32),
        "force_old": scatter_about(key_of[2], (3, NBX, NBY, ATOMS), 1.0, 6.0, ((1, 96), (2, 8)), jnp.float32),
        "counts": plant(jax.random.randint(key_of[3], (NBX, NBY), ATOMS // 2, ATOMS + 1), jax.random.fold_in(key_of[3], 1), ATOMS // 2, ATOMS).astype(jnp.int32),
        "density_coef": jnp.clip(jax.random.uniform(key_of[4], (4,), jnp.float32, 0.02, 0.08), 0.02, 0.08),
        "pair_coef": jnp.clip(jax.random.uniform(key_of[5], (4,), jnp.float32, 0.5, 2.5), 0.5, 2.5),
        "embed_coef": jnp.clip(jax.random.uniform(key_of[6], (2,), jnp.float32, 0.2, 2.0), 0.2, 2.0),
    }


cutoff = 5.5
time_step = 0.004
inverse_mass = 151.83
atom_volume = 11.8
stress_pairs = ((0, 0), (1, 1), (2, 2), (0, 1), (0, 2), (1, 2))
offsets_all = tuple(((first, second) for first in (-1, 0, 1) for second in (-1, 0, 1)))

def poly_value(weight, coeffs):
    nested = coeffs[0] + weight * (coeffs[1] + weight * (coeffs[2] + weight * coeffs[3]))
    return weight * weight * nested

def poly_slope(weight, coeffs):
    nested = coeffs[0] + weight * (coeffs[1] + weight * (coeffs[2] + weight * coeffs[3]))
    rising = coeffs[1] + weight * (2.0 * coeffs[2] + weight * (3.0 * coeffs[3]))
    return 2.0 * weight * nested + weight * weight * rising

def embed_slope(density, coeffs):
    return -0.5 * coeffs[0] / jnp.sqrt(1.0 + density) + 2.0 * coeffs[1] * density

def pair_weight(mine_pos, other_pos, shift_x, shift_y):
    shifts = jnp.array([shift_x * cutoff, shift_y * cutoff, 0.0], dtype=jnp.float32)
    separation = mine_pos[:, :, :, None] - other_pos[:, :, None, :] - shifts[:, None, None, None]
    square = lax.optimization_barrier(jnp.sum(separation * separation, axis=0))
    weight = jnp.maximum(1.0 - square / (cutoff * cutoff), 0.0)
    return (separation, weight)

def make_mask(mine_live, other_live, same_block):
    pair_mask = mine_live[:, :, None] * other_live[:, None, :]
    if same_block:
        atom_count = mine_live.shape[1]
        rows_iota = lax.broadcasted_iota(jnp.int32, (atom_count, atom_count), 0)
        cols_iota = lax.broadcasted_iota(jnp.int32, (atom_count, atom_count), 1)
        pair_mask = pair_mask * (rows_iota != cols_iota).astype(jnp.float32)[None]
    return pair_mask

def tile_terms(mine_block, other_block, shift_x, shift_y, density_coef, pair_coef):
    separation, weight = pair_weight(mine_block[:3], other_block[:3], shift_x, shift_y)
    pair_mask = make_mask(mine_block[3], other_block[3], shift_x == 0 and shift_y == 0)
    strength = ((mine_block[4][:, :, None] + other_block[4][:, None, :]) * poly_slope(weight, density_coef) + poly_slope(weight, pair_coef)) * pair_mask * (2.0 / (cutoff * cutoff))
    pair_force = strength[None] * separation
    products = jnp.stack([separation[first] * pair_force[second] for first, second in stress_pairs]) * (0.5 / atom_volume)
    return (pair_force, products)

def wrap_edges(source):
    source = jnp.concatenate([source[:, -1:], source, source[:, :1]], axis=1)
    return jnp.concatenate([source[:, :, -1:], source, source[:, :, :1]], axis=2)

def reference(position, velocity, force_old, counts, density_coef, pair_coef, embed_coef):
    kick_scale = 0.5 * time_step * inverse_mass
    velocity_half = velocity + kick_scale * force_old
    position_new = position + time_step * velocity_half
    count_x, count_y, atom_count = position.shape[1:]
    alive_mask = (lax.broadcasted_iota(jnp.int32, (count_x, count_y, atom_count), 2) < counts[:, :, None]).astype(jnp.float32)
    group_size = math.gcd(count_y, 64)
    per_row = count_y // group_size
    framed = wrap_edges(jnp.concatenate([position_new, alive_mask[None]], axis=0))
    block_list = jnp.arange(count_x * per_row, dtype=jnp.int32)

    def take_blocks(source, block_index, shift_x, shift_y):
        row_index = block_index // per_row + 1 + shift_x
        start_y = block_index % per_row * group_size + 1 + shift_y
        anchor = jnp.zeros((), jnp.int32)
        window = lax.dynamic_slice(source, (anchor, row_index, start_y, anchor), (source.shape[0], 1, group_size, atom_count))
        return window[:, 0]

    def density_block(block_index):
        mine_block = take_blocks(framed, block_index, 0, 0)
        totals = jnp.zeros((group_size, atom_count), jnp.float32)
        for shift_x, shift_y in offsets_all:
            other_block = take_blocks(framed, block_index, shift_x, shift_y)
            weight = pair_weight(mine_block[:3], other_block[:3], shift_x, shift_y)[1]
            pair_mask = make_mask(mine_block[3], other_block[3], shift_x == 0 and shift_y == 0)
            totals = totals + lax.optimization_barrier(jnp.sum(pair_mask * poly_value(weight, density_coef), axis=2))
        return totals
    density = lax.map(density_block, block_list).reshape(count_x, count_y, atom_count)
    slopes = embed_slope(density, embed_coef)
    full_frame = jnp.concatenate([framed, wrap_edges(slopes[None])], axis=0)

    def force_block(block_index):
        mine_block = take_blocks(full_frame, block_index, 0, 0)
        totals = jnp.zeros((9, group_size, atom_count), jnp.float32)
        for shift_x, shift_y in offsets_all:
            other_block = take_blocks(full_frame, block_index, shift_x, shift_y)
            pair_force, products = tile_terms(mine_block, other_block, shift_x, shift_y, density_coef, pair_coef)
            totals = totals + jnp.concatenate([lax.optimization_barrier(jnp.sum(pair_force, axis=3)), lax.optimization_barrier(jnp.sum(products, axis=3))], axis=0)
        return totals
    combined = lax.map(force_block, block_list)
    combined = combined.transpose(1, 0, 2, 3).reshape(9, count_x, count_y, atom_count)
    forces = combined[:3]
    stress = combined[3:]
    velocity_new = velocity_half + kick_scale * forces
    return (position_new, velocity_new, forces, stress)
```

```python
import functools

import jax
import jax.numpy as jnp
from jax import lax
from jax.experimental import pallas as pl
from jax.experimental.pallas import tpu as pltpu
from jax.sharding import PartitionSpec as P

cutoff = 5.5
time_step = 0.004
inverse_mass = 151.83
atom_volume = 11.8
kick_scale = 0.5 * time_step * inverse_mass
stress_pairs = ((0, 0), (1, 1), (2, 2), (0, 1), (0, 2), (1, 2))
SLOTS = 128
SLOTS_PER_A = 128.0 / 48.0
SLOT_LEAD = 1.5
FAR = 1.0e4
NONE = -1.0e6


def place_kernel(counts_ref, pos_ref, vel_ref, frc_ref, new_ref, half_ref, pay_ref, slot_ref):
    half = [vel_ref[c] + kick_scale * frc_ref[c] for c in range(3)]
    new = [pos_ref[c] + time_step * half[c] for c in range(3)]
    for c in range(3):
        half_ref[c] = half[c]
        new_ref[c] = new[c]
    rows = lax.broadcasted_iota(jnp.int32, (8, SLOTS), 0)
    lane_int = lax.broadcasted_iota(jnp.int32, (8, SLOTS), 1)
    lane = lane_int.astype(jnp.float32)
    count = jnp.zeros((8, SLOTS), jnp.int32)
    for b in range(8):
        count = jnp.where(rows == b, counts_ref[b], count)
    alive = lane_int < count
    wanted = new[2] * SLOTS_PER_A - SLOT_LEAD
    fine = jnp.clip(jnp.floor((wanted + 8.0) * 64.0), 0.0, 16383.0)
    key = jnp.where(alive, fine, 32768.0) * 128.0 + lane
    wanted = jnp.clip(jnp.floor(wanted), 0.0, 127.0)

    def column(values_t, b):
        return jnp.broadcast_to(values_t[:, b : b + 1], (SLOTS, SLOTS))

    key_t = key.T
    ranks = []
    for b in range(8):
        before = column(key_t, b) < key[b : b + 1]
        ranks.append(jnp.sum(jnp.where(before, 1.0, 0.0), axis=0, keepdims=True))
    rank = jnp.concatenate(ranks, axis=0)
    lead = jnp.where(alive, wanted - rank, NONE)
    lead_t = lead.T
    leads = []
    for b in range(8):
        before = column(key_t, b) < key[b : b + 1]
        leads.append(jnp.max(jnp.where(before, column(lead_t, b), NONE), axis=0, keepdims=True))
    slot = rank + jnp.maximum(lead, jnp.concatenate(leads, axis=0))
    slot = jnp.minimum(slot, 128.0 - count.astype(jnp.float32) + rank)
    slot = jnp.where(alive, slot, -1.0)
    slot_ref[...] = slot.astype(jnp.int32)
    slot_t = slot.T
    atom = lax.broadcasted_iota(jnp.int32, (SLOTS, SLOTS), 0).astype(jnp.float32)
    lanes = lax.broadcasted_iota(jnp.int32, (SLOTS, SLOTS), 1).astype(jnp.float32)
    owners = []
    for b in range(8):
        owners.append(
            jnp.max(jnp.where(column(slot_t, b) == lanes, atom, -1.0), axis=0, keepdims=True)
        )
    owner = jnp.concatenate(owners, axis=0)
    taken = owner >= 0.0
    index = jnp.maximum(owner, 0.0).astype(jnp.int32)
    for c in range(3):
        moved = jnp.take_along_axis(new[c], index, axis=1) * (1.0 / cutoff)
        pay_ref[c] = jnp.where(taken, moved, FAR if c == 0 else 0.0)


def pair_kernel(
    dens_ref, pair_ref, emb_ref, mid_ref, low_ref, high_ref, half_ref, slot_ref,
    vel_ref, frc_ref, str_ref,
    near, slopes, packs,
):
    for v in range(3):
        for x in range(6):
            for c in range(3):
                parts = []
                if v < 2:
                    parts.append(low_ref[c, x, v:2])
                parts.append(mid_ref[c, x])
                if v > 0:
                    parts.append(high_ref[c, x, 0:v])
                block = jnp.concatenate(parts, axis=0)
                if c == 1:
                    row = lax.broadcasted_iota(jnp.int32, (6, SLOTS), 0).astype(jnp.float32)
                    block = block + (row + (v - 3.5))
                elif c == 0:
                    block = block + (x - 2.5)
                near[v, c, 6 * x : 6 * x + 6] = block

    most, least = (None, None)
    lane = lax.broadcasted_iota(jnp.int32, (36, SLOTS), 1).astype(jnp.float32)
    for v in (0, 2):
        gap = lane - near[v, 2] * (cutoff * SLOTS_PER_A)
        there = near[v, 0] < 100.0
        high = jnp.where(there, gap, -1.0e6)
        low = jnp.where(there, gap, 1.0e6)
        most = high if most is None else jnp.maximum(most, high)
        least = low if least is None else jnp.minimum(least, low)
    spread = jnp.max(most) - jnp.min(least)
    reach = jnp.clip(spread + (cutoff * SLOTS_PER_A + 0.01), 0.0, 64.0).astype(jnp.int32)
    first = -reach
    last = jnp.minimum(reach, 63) + 1

    a = [dens_ref[k] for k in range(4)]
    p = [pair_ref[k] for k in range(4)]

    def load(v, u, c, m):
        start = 6 * (1 + u) + 8 * m
        return near[v + 1, c, start : start + 8]

    mine = [[load(0, 0, c, m) for c in range(3)] for m in range(3)]

    def density_step(d, totals):
        turn = lax.bitwise_and(d, 127)
        same = jnp.where(d == 0, 100.0, 0.0)
        totals = list(totals)
        for u in (-1, 0, 1):
            for v in (-1, 0, 1):
                for m in range(3):
                    square = None
                    for c in range(3):
                        other = pltpu.roll(load(v, u, c, m), turn, 1)
                        gap = mine[m][c] - other
                        square = gap * gap if square is None else square + gap * gap
                    if u == 0 and v == 0:
                        square = square + same
                    w = jnp.maximum(1.0 - square, 0.0)
                    value = a[0] + w * (a[1] + w * (a[2] + w * a[3]))
                    totals[m] = totals[m] + (w * w) * value
        return tuple(totals)

    zero = jnp.zeros((8, SLOTS), jnp.float32)
    totals = lax.fori_loop(first, last, density_step, (zero,) * 3)
    e0 = emb_ref[0]
    e1 = emb_ref[1]
    for m in range(3):
        slopes[8 * m : 8 * m + 8] = (-0.5 * e0) / jnp.sqrt(1.0 + totals[m]) + (2.0 * e1) * totals[m]

    for u in (-1, 0, 1):
        for v in (-1, 0, 1):
            k = 3 * (u + 1) + v + 1
            for side in range(2):
                for c in range(3):
                    start = 6 * (2 + side + u) + 1
                    packs[k, c, 4 * side : 4 * side + 4] = near[v + 1, c, start : start + 4]
                start = 6 * (1 + side + u) + 1 + v
                packs[k, 3, 4 * side : 4 * side + 4] = slopes[start : start + 4]

    own = [packs[4, c] for c in range(4)]
    gd = [(k + 2.0) * a[k] for k in range(4)]
    gp = [(k + 2.0) * p[k] for k in range(4)]

    def force_step(d, sums):
        turn = lax.bitwise_and(d, 127)
        same = jnp.where(d == 0, 100.0, 0.0)
        sums = list(sums)
        for k in range(9):
            gaps = [own[c] - pltpu.roll(packs[k, c], turn, 1) for c in range(3)]
            square = gaps[0] * gaps[0] + gaps[1] * gaps[1] + gaps[2] * gaps[2]
            if k == 4:
                square = square + same
            w = jnp.maximum(1.0 - square, 0.0)
            slope = own[3] + pltpu.roll(packs[k, 3], turn, 1)
            dens = gd[0] + w * (gd[1] + w * (gd[2] + w * gd[3]))
            pair = gp[0] + w * (gp[1] + w * (gp[2] + w * gp[3]))
            strength = w * (slope * dens + pair)
            pulls = [strength * gap for gap in gaps]
            for c in range(3):
                sums[c] = sums[c] + pulls[c]
            for t, (r, s) in enumerate(stress_pairs):
                sums[3 + t] = sums[3 + t] + gaps[r] * pulls[s]
        return tuple(sums)

    sums = lax.fori_loop(first, last, force_step, (zero,) * 9)
    slot = slot_ref[...]
    alive = slot >= 0
    index = jnp.maximum(slot, 0)

    def restored(values, scale):
        return jnp.where(alive, jnp.take_along_axis(values, index, axis=1) * scale, 0.0)

    for c in range(3):
        force = restored(sums[c], 2.0 / cutoff)
        frc_ref[c] = force
        vel_ref[c] = half_ref[c] + kick_scale * force
    for t in range(6):
        str_ref[t] = restored(sums[3 + t], 1.0 / atom_volume)


def shifted(block, axis, distance):
    count = lax.axis_size(axis)
    route = [(i, (i + distance) % count) for i in range(count)]
    return lax.ppermute(block, axis, route)


def body(position, velocity, force_old, counts, density_coef, pair_coef, embed_coef):
    shape = position.shape
    flat = (3, 8, SLOTS)
    vmem = pl.BlockSpec(memory_space=pltpu.VMEM)
    smem = pl.BlockSpec(memory_space=pltpu.SMEM)
    f32 = jnp.float32
    new, half, pay, slot = pl.pallas_call(
        place_kernel,
        in_specs=[smem, vmem, vmem, vmem],
        out_specs=[vmem] * 4,
        out_shape=[jax.ShapeDtypeStruct(flat, f32)] * 3
        + [jax.ShapeDtypeStruct((8, SLOTS), jnp.int32)],
        name="place",
    )(counts.reshape(8), position.reshape(flat), velocity.reshape(flat), force_old.reshape(flat))
    pay = pay.reshape(shape)
    before = shifted(pay, "gx", 1)
    after = shifted(pay, "gx", -1)
    mid = jnp.concatenate([before, pay, after], axis=1)
    low = shifted(mid[:, :, 2:], "gy", 1)
    high = shifted(mid[:, :, :2], "gy", -1)
    vel, frc, stress = pl.pallas_call(
        pair_kernel,
        in_specs=[smem] * 3 + [vmem] * 5,
        out_specs=[vmem] * 3,
        out_shape=[
            jax.ShapeDtypeStruct(flat, f32),
            jax.ShapeDtypeStruct(flat, f32),
            jax.ShapeDtypeStruct((6, 8, SLOTS), f32),
        ],
        scratch_shapes=[
            pltpu.VMEM((3, 3, 36, SLOTS), f32),
            pltpu.VMEM((24, SLOTS), f32),
            pltpu.VMEM((9, 4, 8, SLOTS), f32),
        ],
        name="pairs",
    )(density_coef, pair_coef, embed_coef, mid, low, high, half, slot)
    return (
        new.reshape(shape),
        vel.reshape(shape),
        frc.reshape(shape),
        stress.reshape((6,) + shape[1:]),
    )


def solution(mesh):
    grid = P(None, "gx", "gy", None)
    return jax.shard_map(
        body,
        mesh=mesh,
        in_specs=(grid, grid, grid, P("gx", "gy"), P(), P(), P()),
        out_specs=(grid, grid, grid, grid),
        check_vma=False,
    )
```

```python
import functools

import jax
import jax.numpy as jnp
from jax import lax
from jax.experimental import pallas as pl
from jax.experimental.pallas import tpu as pltpu
from jax.sharding import PartitionSpec as P

cutoff = 5.5
time_step = 0.004
inverse_mass = 151.83
atom_volume = 11.8
kick_scale = 0.5 * time_step * inverse_mass
stress_pairs = ((0, 0), (1, 1), (2, 2), (0, 1), (0, 2), (1, 2))
SLOTS = 128
SLOTS_PER_A = 128.0 / 48.0
SLOT_LEAD = 1.5
FAR = 1.0e4
NONE = -1.0e6
GRANT = 8 * 2**20


def place_kernel(counts_ref, pos_ref, vel_ref, frc_ref, new_ref, half_ref, pay_ref, slot_ref):
    half = [vel_ref[c] + kick_scale * frc_ref[c] for c in range(3)]
    new = [pos_ref[c] + time_step * half[c] for c in range(3)]
    for c in range(3):
        half_ref[c] = half[c]
        new_ref[c] = new[c]
    rows = lax.broadcasted_iota(jnp.int32, (8, SLOTS), 0)
    lane_int = lax.broadcasted_iota(jnp.int32, (8, SLOTS), 1)
    lane = lane_int.astype(jnp.float32)
    count = jnp.zeros((8, SLOTS), jnp.int32)
    for b in range(8):
        count = jnp.where(rows == b, counts_ref[b // 4, b % 4], count)
    alive = lane_int < count
    wanted = new[2] * SLOTS_PER_A - SLOT_LEAD
    fine = jnp.clip(jnp.floor((wanted + 8.0) * 64.0), 0.0, 16383.0)
    key = jnp.where(alive, fine, 32768.0) * 128.0 + lane
    wanted = jnp.clip(jnp.floor(wanted), 0.0, 127.0)

    def column(values_t, b):
        return jnp.broadcast_to(values_t[:, b : b + 1], (SLOTS, SLOTS))

    key_t = key.T
    ranks = []
    for b in range(8):
        before = column(key_t, b) < key[b : b + 1]
        ranks.append(jnp.sum(jnp.where(before, 1.0, 0.0), axis=0, keepdims=True))
    rank = jnp.concatenate(ranks, axis=0)
    lead = jnp.where(alive, wanted - rank, NONE)
    lead_t = lead.T
    leads = []
    for b in range(8):
        before = column(key_t, b) < key[b : b + 1]
        leads.append(jnp.max(jnp.where(before, column(lead_t, b), NONE), axis=0, keepdims=True))
    slot = rank + jnp.maximum(lead, jnp.concatenate(leads, axis=0))
    slot = jnp.minimum(slot, 128.0 - count.astype(jnp.float32) + rank)
    slot = jnp.where(alive, slot, -1.0)
    slot_ref[...] = slot.astype(jnp.int32)
    slot_t = slot.T
    atom = lax.broadcasted_iota(jnp.int32, (SLOTS, SLOTS), 0).astype(jnp.float32)
    lanes = lax.broadcasted_iota(jnp.int32, (SLOTS, SLOTS), 1).astype(jnp.float32)
    owners = []
    for b in range(8):
        owners.append(
            jnp.max(jnp.where(column(slot_t, b) == lanes, atom, -1.0), axis=0, keepdims=True)
        )
    owner = jnp.concatenate(owners, axis=0)
    taken = owner >= 0.0
    index = jnp.maximum(owner, 0.0).astype(jnp.int32)
    for c in range(3):
        moved = jnp.take_along_axis(new[c], index, axis=1) * (1.0 / cutoff)
        pay_ref[c] = jnp.where(taken, moved, FAR if c == 0 else 0.0)


def reach_of(boxes):
    most, least = (None, None)
    for far, height in boxes:
        lane = lax.broadcasted_iota(jnp.int32, height.shape, 1).astype(jnp.float32)
        gap = lane - height * (cutoff * SLOTS_PER_A)
        there = far < 100.0
        high = jnp.max(jnp.where(there, gap, -1.0e6))
        low = jnp.min(jnp.where(there, gap, 1.0e6))
        most = high if most is None else jnp.maximum(most, high)
        least = low if least is None else jnp.minimum(least, low)
    reach = most - least + (cutoff * SLOTS_PER_A + 0.01)
    return jnp.clip(reach, 0.0, 64.0).astype(jnp.int32)


def offsets_loop(reach, source, turned, step, start):
    rows = source.shape[0]

    def turn(d, ref):
        by = lax.bitwise_and(-d, SLOTS - 1)
        for r in range(0, rows, 8):
            ref[r : r + 8] = pltpu.roll(source[r : r + 8], by, 1)

    def pair(i, carry):
        d = 2 * i - reach
        turn(d + 1, turned.at[1])
        carry = step(d, turned.at[0], carry)
        turn(d + 2, turned.at[0])
        return step(d + 1, turned.at[1], carry)

    turn(-reach, turned.at[0])
    return lax.fori_loop(0, jnp.minimum(reach + 1, SLOTS // 2), pair, start)


def density_term(square, a):
    w = jnp.maximum(1.0 - square, 0.0)
    value = a[0] + w * (a[1] + w * (a[2] + w * a[3]))
    return (w * w) * value


def square_of(mine, others):
    gaps = [m - o for m, o in zip(mine, others)]
    return gaps[0] * gaps[0] + gaps[1] * gaps[1] + gaps[2] * gaps[2]


def early_kernel(dens_ref, pair_ref, emb_ref, mid_ref, sum_ref, coef_ref, source, turned):
    for k in range(4):
        coef_ref[k : k + 1] = jnp.full((1, SLOTS), dens_ref[k], jnp.float32)
        coef_ref[4 + k : 5 + k] = jnp.full((1, SLOTS), pair_ref[k], jnp.float32)
    for k in range(2):
        coef_ref[8 + k : 9 + k] = jnp.full((1, SLOTS), emb_ref[k], jnp.float32)
    boxes = []
    for x in range(6):
        boxes.append((mid_ref[0, x], mid_ref[2, x]))
        for v in range(3):
            for c in range(3):
                base = 24 * (3 * v + c) + 4 * x
                low = max(0, 1 - v)
                high = min(4, 5 - v)
                block = mid_ref[c, x, low + v - 1 : high + v - 1]
                row = lax.broadcasted_iota(jnp.int32, block.shape, 0).astype(jnp.float32)
                block = block + (x - 2.5, row + (low + v - 2.5), 0.0)[c]
                source[base + low : base + high] = block
                for edge in (0,) * low + (3,) * (4 - high):
                    source[base + edge : base + edge + 1] = jnp.full((1, SLOTS), FAR, jnp.float32)
    a = [dens_ref[k] for k in range(4)]

    def rows_of(ref, u, v, c, m):
        start = 24 * (3 * (v + 1) + c) + 4 * (1 + u) + 8 * m
        return ref[start : start + 8]

    mine = [[rows_of(source, 0, 0, c, m) for c in range(3)] for m in range(2)]

    def step(d, ref, totals):
        same = jnp.where(d == 0, 100.0, 0.0)
        totals = list(totals)
        for u in (-1, 0, 1):
            for v in (-1, 0, 1):
                for m in range(2):
                    square = square_of(mine[m], [rows_of(ref, u, v, c, m) for c in range(3)])
                    if u == 0 and v == 0:
                        square = square + same
                    totals[m] = totals[m] + density_term(square, a)
        return tuple(totals)

    zero = jnp.zeros((8, SLOTS), jnp.float32)
    totals = offsets_loop(reach_of(boxes), source, turned, step, (zero, zero))
    for m in range(2):
        sum_ref[8 * m : 8 * m + 8] = totals[m]


def late_kernel(
    mid_ref, low_ref, high_ref, half_ref, slot_ref, sum_ref, coef_ref,
    vel_ref, frc_ref, str_ref,
    rims, rims_turned, edges, slopes, packs, packs_turned,
):
    f32 = jnp.float32

    def block_row(c, x, y):
        if y < 2:
            values = low_ref[c, x, y : y + 1]
        elif y < 6:
            values = mid_ref[c, x, y - 2 : y - 1]
        else:
            values = high_ref[c, x, y - 6 : y - 5]
        return values + (x - 2.5, y - 3.5, 0.0)[c]

    for v in range(3):
        for c in range(3):
            for x in range(6):
                for s in range(2):
                    row = 12 * (3 * v + c) + 2 * x + s
                    rims[row : row + 1] = block_row(c, x, (1, 6)[s] + v - 1)
    boxes = []
    for x in range(6):
        boxes.append((mid_ref[0, x], mid_ref[2, x]))
        boxes.append((low_ref[0, x], low_ref[2, x]))
        boxes.append((high_ref[0, x], high_ref[2, x]))
    reach = reach_of(boxes)

    def coef(k):
        return jnp.broadcast_to(coef_ref[k : k + 1], (8, SLOTS))

    a = [coef(k) for k in range(4)]
    p = [coef(4 + k) for k in range(4)]

    def rim(ref, u, v, c):
        start = 12 * (3 * (v + 1) + c) + 2 * (1 + u)
        return ref[start : start + 8]

    outer = [rim(rims, 0, 0, c) for c in range(3)]
    for c in range(3):
        for x in range(4):
            for s in range(2):
                edges[c, 2 * x + s : 2 * x + s + 1] = block_row(c, x + 1, (2, 5)[s])
    inner = [edges[c] for c in range(3)]

    def density_step(d, ref, totals):
        same = jnp.where(d == 0, 100.0, 0.0)
        out, inn = totals
        for u in (-1, 0, 1):
            for v in (-1, 0, 1):
                others = [rim(ref, u, v, c) for c in range(3)]
                square = square_of(outer, others)
                if u == 0 and v == 0:
                    square = square + same
                out = out + density_term(square, a)
                if v == 0:
                    inn = inn + density_term(square_of(inner, others), a)
        return (out, inn)

    zero = jnp.zeros((8, SLOTS), f32)
    out, inn = offsets_loop(reach, rims, rims_turned, density_step, (zero, zero))
    edges[0] = out
    edges[1] = inn
    for x in range(4):
        for s in range(2):
            row = 2 * x + s
            slopes[6 * x + 5 * s : 6 * x + 5 * s + 1] = edges[0, row : row + 1]
            mine = 4 * x + 3 * s
            slopes[6 * x + 3 * s + 1 : 6 * x + 3 * s + 2] = (
                sum_ref[mine : mine + 1] + edges[1, row : row + 1]
            )
        slopes[6 * x + 2 : 6 * x + 4] = sum_ref[4 * x + 1 : 4 * x + 3]
    for m in range(3):
        total = slopes[8 * m : 8 * m + 8]
        slopes[8 * m : 8 * m + 8] = (-0.5 * coef(8)) / jnp.sqrt(1.0 + total) + (
            2.0 * coef(9)
        ) * total

    for u in (-1, 0, 1):
        for v in (-1, 0, 1):
            k = 3 * (u + 1) + v + 1
            for s in range(2):
                x = 2 + s + u
                for c in range(3):
                    base = 8 * (4 * k + c) + 4 * s
                    for y in range(2 + v, 6 + v):
                        if y in (1, 6):
                            packs[base + y - 2 - v : base + y - 1 - v] = block_row(c, x, y)
                    first = max(2, 2 + v)
                    last = min(6, 6 + v)
                    block = mid_ref[c, x, first - 2 : last - 2]
                    row = lax.broadcasted_iota(jnp.int32, block.shape, 0).astype(f32)
                    block = block + (x - 2.5, row + (first - 3.5), 0.0)[c]
                    packs[base + first - 2 - v : base + last - 2 - v] = block
                base = 8 * (4 * k + 3) + 4 * s
                start = 6 * (x - 1) + 1 + v
                packs[base : base + 4] = slopes[start : start + 4]

    def member(ref, k, c):
        return ref[8 * (4 * k + c) : 8 * (4 * k + c) + 8]

    own = [member(packs, 4, c) for c in range(4)]
    gd = [(k + 2.0) * a[k] for k in range(4)]
    gp = [(k + 2.0) * p[k] for k in range(4)]

    def force_step(d, ref, sums):
        same = jnp.where(d == 0, 100.0, 0.0)
        sums = list(sums)
        for k in range(9):
            gaps = [own[c] - member(ref, k, c) for c in range(3)]
            square = gaps[0] * gaps[0] + gaps[1] * gaps[1] + gaps[2] * gaps[2]
            if k == 4:
                square = square + same
            w = jnp.maximum(1.0 - square, 0.0)
            slope = own[3] + member(ref, k, 3)
            dens = gd[0] + w * (gd[1] + w * (gd[2] + w * gd[3]))
            pair = gp[0] + w * (gp[1] + w * (gp[2] + w * gp[3]))
            strength = w * (slope * dens + pair)
            pulls = [strength * gap for gap in gaps]
            for c in range(3):
                sums[c] = sums[c] + pulls[c]
            for t, (r, s) in enumerate(stress_pairs):
                sums[3 + t] = sums[3 + t] + gaps[r] * pulls[s]
        return tuple(sums)

    sums = offsets_loop(reach, packs, packs_turned, force_step, (zero,) * 9)
    slot = slot_ref[...]
    alive = slot >= 0
    index = jnp.maximum(slot, 0)

    def restored(values, scale):
        return jnp.where(alive, jnp.take_along_axis(values, index, axis=1) * scale, 0.0)

    for c in range(3):
        force = restored(sums[c], 2.0 / cutoff)
        frc_ref[c] = force
        vel_ref[c] = half_ref[c] + kick_scale * force
    for t in range(6):
        str_ref[t] = restored(sums[3 + t], 1.0 / atom_volume)


def shifted(block, axis, distance):
    count = lax.axis_size(axis)
    route = [(i, (i + distance) % count) for i in range(count)]
    return lax.ppermute(block, axis, route)


def body(position, velocity, force_old, counts, density_coef, pair_coef, embed_coef):
    shape = position.shape
    flat = (3, 8, SLOTS)
    vmem = pl.BlockSpec(memory_space=pltpu.VMEM)
    smem = pl.BlockSpec(memory_space=pltpu.SMEM)
    f32 = jnp.float32
    new, half, pay, slot = pl.pallas_call(
        place_kernel,
        in_specs=[smem, vmem, vmem, vmem],
        out_specs=[vmem] * 4,
        out_shape=[jax.ShapeDtypeStruct(flat, f32)] * 3
        + [jax.ShapeDtypeStruct((8, SLOTS), jnp.int32)],
        compiler_params=pltpu.CompilerParams(vmem_limit_bytes=GRANT),
        name="place",
    )(counts, position.reshape(flat), velocity.reshape(flat), force_old.reshape(flat))
    pay = pay.reshape(shape)
    after = shifted(pay, "gx", -1)
    before = shifted(pay, "gx", 1)
    mid = jnp.concatenate([before, pay, after], axis=1)
    high = shifted(mid[:, :, :2], "gy", -1)
    low = shifted(mid[:, :, 2:], "gy", 1)
    total, coefs = pl.pallas_call(
        early_kernel,
        in_specs=[smem] * 3 + [vmem],
        out_specs=[vmem] * 2,
        out_shape=[jax.ShapeDtypeStruct((16, SLOTS), f32)] * 2,
        scratch_shapes=[pltpu.VMEM((216, SLOTS), f32), pltpu.VMEM((2, 216, SLOTS), f32)],
        cost_estimate=pl.CostEstimate(flops=12000000, bytes_accessed=60000, transcendentals=0),
        compiler_params=pltpu.CompilerParams(vmem_limit_bytes=GRANT),
        name="early",
    )(density_coef, pair_coef, embed_coef, mid)
    vel, frc, stress = pl.pallas_call(
        late_kernel,
        in_specs=[vmem] * 7,
        out_specs=[vmem] * 3,
        out_shape=[
            jax.ShapeDtypeStruct(flat, f32),
            jax.ShapeDtypeStruct(flat, f32),
            jax.ShapeDtypeStruct((6, 8, SLOTS), f32),
        ],
        scratch_shapes=[
            pltpu.VMEM((112, SLOTS), f32),
            pltpu.VMEM((2, 112, SLOTS), f32),
            pltpu.VMEM((3, 8, SLOTS), f32),
            pltpu.VMEM((24, SLOTS), f32),
            pltpu.VMEM((288, SLOTS), f32),
            pltpu.VMEM((2, 288, SLOTS), f32),
        ],
        compiler_params=pltpu.CompilerParams(vmem_limit_bytes=GRANT),
        name="late",
    )(mid, low, high, half, slot, total, coefs)
    return (
        new.reshape(shape),
        vel.reshape(shape),
        frc.reshape(shape),
        stress.reshape((6,) + shape[1:]),
    )


def solution(mesh):
    grid = P(None, "gx", "gy", None)
    return jax.shard_map(
        body,
        mesh=mesh,
        in_specs=(grid, grid, grid, P("gx", "gy"), P(), P(), P()),
        out_specs=(grid, grid, grid, grid),
        check_vma=False,
    )
```

```python
import jax
import jax.numpy as jnp
from jax import lax
from jax.experimental import pallas as pl
from jax.experimental.pallas import tpu as pltpu
from jax.sharding import PartitionSpec as P


cutoff = 5.5
time_step = 0.004
inverse_mass = 151.83
atom_volume = 11.8
kick_scale = 0.5 * time_step * inverse_mass
stress_pairs = ((0, 0), (1, 1), (2, 2), (0, 1), (0, 2), (1, 2))
SLOTS = 128
SLOTS_PER_A = 128.0 / 48.0
SLOT_LEAD = 1.5
FAR = 1.0e4
NONE = -1.0e6
GRANT = 8 * 2**20


def place_kernel(
    counts_hbm, pos_hbm, vel_hbm, frc_hbm,
    new_ref, half_ref, pay_ref, slot_ref,
    fetched, counts_ref, arrived,
):
    copies = [
        pltpu.make_async_copy(source, fetched.at[k], arrived.at[k])
        for k, source in enumerate((pos_hbm, vel_hbm, frc_hbm))
    ]
    copies.append(pltpu.make_async_copy(counts_hbm, counts_ref, arrived.at[3]))
    for copy in copies:
        copy.start()
    for copy in copies:
        copy.wait()
    pos_ref, vel_ref, frc_ref = [fetched.at[k] for k in range(3)]
    half = [vel_ref[c] + kick_scale * frc_ref[c] for c in range(3)]
    new = [pos_ref[c] + time_step * half[c] for c in range(3)]
    for c in range(3):
        half_ref[c] = half[c]
        new_ref[c] = new[c]
    rows = lax.broadcasted_iota(jnp.int32, (8, SLOTS), 0)
    lane_int = lax.broadcasted_iota(jnp.int32, (8, SLOTS), 1)
    lane = lane_int.astype(jnp.float32)
    count = jnp.zeros((8, SLOTS), jnp.int32)
    for b in range(8):
        count = jnp.where(rows == b, counts_ref[b // 4, b % 4], count)
    alive = lane_int < count
    wanted = new[2] * SLOTS_PER_A - SLOT_LEAD
    fine = jnp.clip(jnp.floor((wanted + 8.0) * 64.0), 0.0, 16383.0)
    key = jnp.where(alive, fine, 32768.0) * 128.0 + lane
    wanted = jnp.clip(jnp.floor(wanted), 0.0, 127.0)

    def column(values_t, b):
        return jnp.broadcast_to(values_t[:, b : b + 1], (SLOTS, SLOTS))

    key_t = key.T
    ranks = []
    for b in range(8):
        before = column(key_t, b) < key[b : b + 1]
        ranks.append(jnp.sum(jnp.where(before, 1.0, 0.0), axis=0, keepdims=True))
    rank = jnp.concatenate(ranks, axis=0)
    lead = jnp.where(alive, wanted - rank, NONE)
    lead_t = lead.T
    leads = []
    for b in range(8):
        before = column(key_t, b) < key[b : b + 1]
        leads.append(jnp.max(jnp.where(before, column(lead_t, b), NONE), axis=0, keepdims=True))
    slot = rank + jnp.maximum(lead, jnp.concatenate(leads, axis=0))
    slot = jnp.minimum(slot, 128.0 - count.astype(jnp.float32) + rank)
    slot = jnp.where(alive, slot, -1.0)
    slot_ref[...] = slot.astype(jnp.int32)
    slot_t = slot.T
    atom = lax.broadcasted_iota(jnp.int32, (SLOTS, SLOTS), 0).astype(jnp.float32)
    lanes = lax.broadcasted_iota(jnp.int32, (SLOTS, SLOTS), 1).astype(jnp.float32)
    owners = []
    for b in range(8):
        owners.append(
            jnp.max(jnp.where(column(slot_t, b) == lanes, atom, -1.0), axis=0, keepdims=True)
        )
    owner = jnp.concatenate(owners, axis=0)
    taken = owner >= 0.0
    index = jnp.maximum(owner, 0.0).astype(jnp.int32)
    for c in range(3):
        moved = jnp.take_along_axis(new[c], index, axis=1) * (1.0 / cutoff)
        pay_ref[c] = jnp.where(taken, moved, FAR if c == 0 else 0.0)


def reach_of(boxes):
    most, least = (None, None)
    for far, height in boxes:
        lane = lax.broadcasted_iota(jnp.int32, height.shape, 1).astype(jnp.float32)
        gap = lane - height * (cutoff * SLOTS_PER_A)
        there = far < 100.0
        high = jnp.max(jnp.where(there, gap, -1.0e6))
        low = jnp.min(jnp.where(there, gap, 1.0e6))
        most = high if most is None else jnp.maximum(most, high)
        least = low if least is None else jnp.minimum(least, low)
    reach = most - least + (cutoff * SLOTS_PER_A + 0.01)
    return jnp.clip(reach, 0.0, 64.0).astype(jnp.int32)


def offsets_loop(reach, source, turned, step, start):
    rows = source.shape[0]

    def turn(d, ref):
        by = lax.bitwise_and(-d, SLOTS - 1)
        for r in range(0, rows, 8):
            ref[r : r + 8] = pltpu.roll(source[r : r + 8], by, 1)

    def pair(i, carry):
        d = 2 * i - reach
        turn(d + 1, turned.at[1])
        carry = step(d, turned.at[0], carry)
        turn(d + 2, turned.at[0])
        return step(d + 1, turned.at[1], carry)

    turn(-reach, turned.at[0])
    return lax.fori_loop(0, jnp.minimum(reach + 1, SLOTS // 2), pair, start)


def monic(coefs):
    return [c / coefs[3] for c in coefs[:3]]


def cubic(w, m):
    return m[0] + w * (m[1] + w * (m[2] + w))


def density_term(square, m):
    w = jnp.maximum(1.0 - square, 0.0)
    return (w * w) * cubic(w, m)


def square_of(mine, others):
    gaps = [m - o for m, o in zip(mine, others)]
    return gaps[0] * gaps[0] + gaps[1] * gaps[1] + gaps[2] * gaps[2]


def early_kernel(dens_ref, pair_ref, emb_ref, mid_ref, sum_ref, coef_ref, source, turned):
    for k in range(4):
        coef_ref[k : k + 1] = jnp.full((1, SLOTS), dens_ref[k], jnp.float32)
        coef_ref[4 + k : 5 + k] = jnp.full((1, SLOTS), pair_ref[k], jnp.float32)
    for k in range(2):
        coef_ref[8 + k : 9 + k] = jnp.full((1, SLOTS), emb_ref[k], jnp.float32)
    boxes = []
    for x in range(6):
        boxes.append((mid_ref[0, x], mid_ref[2, x]))
        for v in range(3):
            for c in range(3):
                base = 24 * (3 * v + c) + 4 * x
                low = max(0, 1 - v)
                high = min(4, 5 - v)
                block = mid_ref[c, x, low + v - 1 : high + v - 1]
                row = lax.broadcasted_iota(jnp.int32, block.shape, 0).astype(jnp.float32)
                block = block + (x - 2.5, row + (low + v - 2.5), 0.0)[c]
                source[base + low : base + high] = block
                for edge in (0,) * low + (3,) * (4 - high):
                    source[base + edge : base + edge + 1] = jnp.full((1, SLOTS), FAR, jnp.float32)
    a = monic([jnp.full((8, SLOTS), dens_ref[k], jnp.float32) for k in range(4)])

    def rows_of(ref, u, v, c, m):
        start = 24 * (3 * (v + 1) + c) + 4 * (1 + u) + 8 * m
        return ref[start : start + 8]

    mine = [[rows_of(source, 0, 0, c, m) for c in range(3)] for m in range(2)]

    def step(d, ref, totals):
        same = jnp.where(d == 0, 100.0, 0.0)
        totals = list(totals)
        for u in (-1, 0, 1):
            for v in (-1, 0, 1):
                for m in range(2):
                    square = square_of(mine[m], [rows_of(ref, u, v, c, m) for c in range(3)])
                    if u == 0 and v == 0:
                        square = square + same
                    totals[m] = totals[m] + density_term(square, a)
        return tuple(totals)

    zero = jnp.zeros((8, SLOTS), jnp.float32)
    totals = offsets_loop(reach_of(boxes), source, turned, step, (zero, zero))
    for m in range(2):
        sum_ref[8 * m : 8 * m + 8] = totals[m]


def late_kernel(
    mid_ref, low_ref, high_ref, half_ref, slot_ref, sum_ref, coef_ref,
    vel_ref, frc_ref, str_ref,
    rims, rims_turned, edges, slopes, packs, packs_turned,
):
    f32 = jnp.float32

    def block_row(c, x, y):
        if y < 2:
            values = low_ref[c, x, y : y + 1]
        elif y < 6:
            values = mid_ref[c, x, y - 2 : y - 1]
        else:
            values = high_ref[c, x, y - 6 : y - 5]
        return values + (x - 2.5, y - 3.5, 0.0)[c]

    for v in range(3):
        for c in range(3):
            for x in range(6):
                for s in range(2):
                    row = 12 * (3 * v + c) + 2 * x + s
                    rims[row : row + 1] = block_row(c, x, (1, 6)[s] + v - 1)
    boxes = []
    for x in range(6):
        boxes.append((mid_ref[0, x], mid_ref[2, x]))
        boxes.append((low_ref[0, x], low_ref[2, x]))
        boxes.append((high_ref[0, x], high_ref[2, x]))
    reach = reach_of(boxes)

    def coef(k):
        return jnp.broadcast_to(coef_ref[k : k + 1], (8, SLOTS))

    a = [coef(k) for k in range(4)]
    p = [coef(4 + k) for k in range(4)]
    am = monic(a)

    def rim(ref, u, v, c):
        start = 12 * (3 * (v + 1) + c) + 2 * (1 + u)
        return ref[start : start + 8]

    outer = [rim(rims, 0, 0, c) for c in range(3)]
    for c in range(3):
        for x in range(4):
            for s in range(2):
                edges[c, 2 * x + s : 2 * x + s + 1] = block_row(c, x + 1, (2, 5)[s])
    inner = [edges[c] for c in range(3)]

    def density_step(d, ref, totals):
        same = jnp.where(d == 0, 100.0, 0.0)
        out, inn = totals
        for u in (-1, 0, 1):
            for v in (-1, 0, 1):
                others = [rim(ref, u, v, c) for c in range(3)]
                square = square_of(outer, others)
                if u == 0 and v == 0:
                    square = square + same
                out = out + density_term(square, am)
                if v == 0:
                    inn = inn + density_term(square_of(inner, others), am)
        return (out, inn)

    zero = jnp.zeros((8, SLOTS), f32)
    out, inn = offsets_loop(reach, rims, rims_turned, density_step, (zero, zero))
    edges[0] = out
    edges[1] = inn
    for x in range(4):
        for s in range(2):
            row = 2 * x + s
            slopes[6 * x + 5 * s : 6 * x + 5 * s + 1] = edges[0, row : row + 1]
            mine = 4 * x + 3 * s
            slopes[6 * x + 3 * s + 1 : 6 * x + 3 * s + 2] = (
                sum_ref[mine : mine + 1] + edges[1, row : row + 1]
            )
        slopes[6 * x + 2 : 6 * x + 4] = sum_ref[4 * x + 1 : 4 * x + 3]
    for m in range(3):
        total = slopes[8 * m : 8 * m + 8] * a[3]
        slope = (-0.5 * coef(8)) / jnp.sqrt(1.0 + total) + (2.0 * coef(9)) * total
        slopes[8 * m : 8 * m + 8] = slope * (a[3] / p[3])

    for u in (-1, 0, 1):
        for v in (-1, 0, 1):
            k = 3 * (u + 1) + v + 1
            for s in range(2):
                x = 2 + s + u
                for c in range(3):
                    base = 8 * (4 * k + c) + 4 * s
                    for y in range(2 + v, 6 + v):
                        if y in (1, 6):
                            packs[base + y - 2 - v : base + y - 1 - v] = block_row(c, x, y)
                    first = max(2, 2 + v)
                    last = min(6, 6 + v)
                    block = mid_ref[c, x, first - 2 : last - 2]
                    row = lax.broadcasted_iota(jnp.int32, block.shape, 0).astype(f32)
                    block = block + (x - 2.5, row + (first - 3.5), 0.0)[c]
                    packs[base + first - 2 - v : base + last - 2 - v] = block
                base = 8 * (4 * k + 3) + 4 * s
                start = 6 * (x - 1) + 1 + v
                packs[base : base + 4] = slopes[start : start + 4]

    def member(ref, k, c):
        return ref[8 * (4 * k + c) : 8 * (4 * k + c) + 8]

    own = [member(packs, 4, c) for c in range(4)]
    gd = monic([(k + 2.0) * a[k] for k in range(4)])
    gp = monic([(k + 2.0) * p[k] for k in range(4)])

    def force_step(d, ref, sums):
        same = jnp.where(d == 0, 100.0, 0.0)
        sums = list(sums)
        for k in range(9):
            gaps = [own[c] - member(ref, k, c) for c in range(3)]
            square = gaps[0] * gaps[0] + gaps[1] * gaps[1] + gaps[2] * gaps[2]
            if k == 4:
                square = square + same
            w = jnp.maximum(1.0 - square, 0.0)
            slope = own[3] + member(ref, k, 3)
            strength = w * (slope * cubic(w, gd) + cubic(w, gp))
            pulls = [strength * gap for gap in gaps]
            for c in range(3):
                sums[c] = sums[c] + pulls[c]
            for t, (r, s) in enumerate(stress_pairs):
                sums[3 + t] = sums[3 + t] + gaps[r] * pulls[s]
        return tuple(sums)

    sums = offsets_loop(reach, packs, packs_turned, force_step, (zero,) * 9)
    slot = slot_ref[...]
    alive = slot >= 0
    index = jnp.maximum(slot, 0)

    def restored(values, scale):
        moved = jnp.take_along_axis(values, index, axis=1)
        return jnp.where(alive, moved * (scale * p[3]), 0.0)

    for c in range(3):
        force = restored(sums[c], 10.0 / cutoff)
        frc_ref[c] = force
        vel_ref[c] = half_ref[c] + kick_scale * force
    for t in range(6):
        str_ref[t] = restored(sums[3 + t], 5.0 / atom_volume)


def shifted(block, axis, distance):
    count = lax.axis_size(axis)
    route = [(i, (i + distance) % count) for i in range(count)]
    return lax.ppermute(block, axis, route)


def body(position, velocity, force_old, counts, density_coef, pair_coef, embed_coef):
    shape = position.shape
    flat = (3, 8, SLOTS)
    vmem = pl.BlockSpec(memory_space=pltpu.VMEM)
    smem = pl.BlockSpec(memory_space=pltpu.SMEM)
    hbm = pl.BlockSpec(memory_space=pltpu.HBM)
    f32 = jnp.float32
    new, half, pay, slot = pl.pallas_call(
        place_kernel,
        in_specs=[hbm] * 4,
        out_specs=[vmem] * 4,
        out_shape=[jax.ShapeDtypeStruct(flat, f32)] * 3
        + [jax.ShapeDtypeStruct((8, SLOTS), jnp.int32)],
        scratch_shapes=[
            pltpu.VMEM((3,) + flat, f32),
            pltpu.SMEM(counts.shape, jnp.int32),
            pltpu.SemaphoreType.DMA((4,)),
        ],
        compiler_params=pltpu.CompilerParams(vmem_limit_bytes=GRANT),
        name="place",
    )(
        *[
            pltpu.with_memory_space_constraint(source, pltpu.HBM)
            for source in (
                counts,
                position.reshape(flat),
                velocity.reshape(flat),
                force_old.reshape(flat),
            )
        ],
    )
    pay = pay.reshape(shape)
    before = shifted(pay, "gx", 1)
    after = shifted(pay, "gx", -1)
    mid = jnp.concatenate([before, pay, after], axis=1)
    high = shifted(mid[:, :, :2], "gy", -1)
    low = shifted(mid[:, :, 2:], "gy", 1)
    total, coefs = pl.pallas_call(
        early_kernel,
        in_specs=[smem] * 3 + [vmem],
        out_specs=[vmem] * 2,
        out_shape=[jax.ShapeDtypeStruct((16, SLOTS), f32)] * 2,
        scratch_shapes=[pltpu.VMEM((216, SLOTS), f32), pltpu.VMEM((2, 216, SLOTS), f32)],
        cost_estimate=pl.CostEstimate(flops=12000000, bytes_accessed=60000, transcendentals=0),
        compiler_params=pltpu.CompilerParams(vmem_limit_bytes=GRANT),
        name="early",
    )(density_coef, pair_coef, embed_coef, mid)
    vel, frc, stress = pl.pallas_call(
        late_kernel,
        in_specs=[vmem] * 7,
        out_specs=[vmem] * 3,
        out_shape=[
            jax.ShapeDtypeStruct(flat, f32),
            jax.ShapeDtypeStruct(flat, f32),
            jax.ShapeDtypeStruct((6, 8, SLOTS), f32),
        ],
        scratch_shapes=[
            pltpu.VMEM((112, SLOTS), f32),
            pltpu.VMEM((2, 112, SLOTS), f32),
            pltpu.VMEM((3, 8, SLOTS), f32),
            pltpu.VMEM((24, SLOTS), f32),
            pltpu.VMEM((288, SLOTS), f32),
            pltpu.VMEM((2, 288, SLOTS), f32),
        ],
        compiler_params=pltpu.CompilerParams(vmem_limit_bytes=GRANT),
        name="late",
    )(mid, low, high, half, slot, total, coefs)
    return (
        new.reshape(shape),
        vel.reshape(shape),
        frc.reshape(shape),
        stress.reshape((6,) + shape[1:]),
    )


def solution(mesh):
    grid = P(None, "gx", "gy", None)
    return jax.shard_map(
        body,
        mesh=mesh,
        in_specs=(grid, grid, grid, P("gx", "gy"), P(), P(), P()),
        out_specs=(grid, grid, grid, grid),
        check_vma=False,
    )
```

```python
import jax
import jax.numpy as jnp
from jax import lax
from jax.experimental import pallas as pl
from jax.experimental.pallas import tpu as pltpu
from jax.sharding import PartitionSpec as P


cutoff = 5.5
time_step = 0.004
inverse_mass = 151.83
atom_volume = 11.8
kick_scale = 0.5 * time_step * inverse_mass
stress_pairs = ((0, 0), (1, 1), (2, 2), (0, 1), (0, 2), (1, 2))
SLOTS = 128
SLOTS_PER_A = 128.0 / 48.0
SLOT_LEAD = 1.5
FAR = 1.0e4
NONE = -1.0e6
GRANT = 8 * 2**20


def place_kernel(
    counts_hbm, pos_hbm, vel_hbm, frc_hbm,
    new_ref, half_ref, pay_ref, slot_ref,
    fetched, counts_ref, arrived,
):
    copies = [
        pltpu.make_async_copy(source, fetched.at[k], arrived.at[k])
        for k, source in enumerate((pos_hbm, vel_hbm, frc_hbm))
    ]
    copies.append(pltpu.make_async_copy(counts_hbm, counts_ref, arrived.at[3]))
    for copy in copies:
        copy.start()
    for copy in copies:
        copy.wait()
    pos_ref, vel_ref, frc_ref = [fetched.at[k] for k in range(3)]
    half = [vel_ref[c] + kick_scale * frc_ref[c] for c in range(3)]
    new = [pos_ref[c] + time_step * half[c] for c in range(3)]
    for c in range(3):
        half_ref[c] = half[c]
        new_ref[c] = new[c]
    rows = lax.broadcasted_iota(jnp.int32, (8, SLOTS), 0)
    lane_int = lax.broadcasted_iota(jnp.int32, (8, SLOTS), 1)
    lane = lane_int.astype(jnp.float32)
    count = jnp.zeros((8, SLOTS), jnp.int32)
    for b in range(8):
        count = jnp.where(rows == b, counts_ref[b // 4, b % 4], count)
    alive = lane_int < count
    wanted = new[2] * SLOTS_PER_A - SLOT_LEAD
    fine = jnp.clip(jnp.floor((wanted + 8.0) * 64.0), 0.0, 16383.0)
    key = jnp.where(alive, fine, 32768.0) * 128.0 + lane
    wanted = jnp.clip(jnp.floor(wanted), 0.0, 127.0)

    def column(values_t, b):
        return jnp.broadcast_to(values_t[:, b : b + 1], (SLOTS, SLOTS))

    key_t = key.T
    ranks = []
    for b in range(8):
        before = column(key_t, b) < key[b : b + 1]
        ranks.append(jnp.sum(jnp.where(before, 1.0, 0.0), axis=0, keepdims=True))
    rank = jnp.concatenate(ranks, axis=0)
    lead = jnp.where(alive, wanted - rank, NONE)
    lead_t = lead.T
    leads = []
    for b in range(8):
        before = column(key_t, b) < key[b : b + 1]
        leads.append(jnp.max(jnp.where(before, column(lead_t, b), NONE), axis=0, keepdims=True))
    slot = rank + jnp.maximum(lead, jnp.concatenate(leads, axis=0))
    slot = jnp.minimum(slot, 128.0 - count.astype(jnp.float32) + rank)
    slot = jnp.where(alive, slot, -1.0)
    slot_ref[...] = slot.astype(jnp.int32)
    slot_t = slot.T
    atom = lax.broadcasted_iota(jnp.int32, (SLOTS, SLOTS), 0).astype(jnp.float32)
    lanes = lax.broadcasted_iota(jnp.int32, (SLOTS, SLOTS), 1).astype(jnp.float32)
    owners = []
    for b in range(8):
        owners.append(
            jnp.max(jnp.where(column(slot_t, b) == lanes, atom, -1.0), axis=0, keepdims=True)
        )
    owner = jnp.concatenate(owners, axis=0)
    taken = owner >= 0.0
    index = jnp.maximum(owner, 0.0).astype(jnp.int32)
    for c in range(3):
        moved = jnp.take_along_axis(new[c], index, axis=1) * (1.0 / cutoff)
        pay_ref[c] = jnp.where(taken, moved, FAR if c == 0 else 0.0)


def reach_of(boxes):
    most, least = (None, None)
    for far, height in boxes:
        lane = lax.broadcasted_iota(jnp.int32, height.shape, 1).astype(jnp.float32)
        gap = lane - height * (cutoff * SLOTS_PER_A)
        there = far < 100.0
        high = jnp.max(jnp.where(there, gap, -1.0e6))
        low = jnp.min(jnp.where(there, gap, 1.0e6))
        most = high if most is None else jnp.maximum(most, high)
        least = low if least is None else jnp.minimum(least, low)
    reach = most - least + (cutoff * SLOTS_PER_A + 0.01)
    return jnp.clip(reach, 0.0, 64.0).astype(jnp.int32)


def offsets_loop(reach, source, turned, step, start):
    rows = source.shape[0]

    def turn(d, ref):
        by = lax.bitwise_and(-d, SLOTS - 1)
        for r in range(0, rows, 8):
            ref[r : r + 8] = pltpu.roll(source[r : r + 8], by, 1)

    def pair(i, carry):
        d = 2 * i - reach
        turn(d + 1, turned.at[1])
        carry = step(d, turned.at[0], carry)
        turn(d + 2, turned.at[0])
        return step(d + 1, turned.at[1], carry)

    turn(-reach, turned.at[0])
    return lax.fori_loop(0, jnp.minimum(reach + 1, SLOTS // 2), pair, start)


def monic(coefs):
    return [c / coefs[3] for c in coefs[:3]]


def cubic(w, m):
    return m[0] + w * (m[1] + w * (m[2] + w))


def density_term(square, m):
    w = jnp.maximum(1.0 - square, 0.0)
    return (w * w) * cubic(w, m)


def square_of(mine, others):
    gaps = [m - o for m, o in zip(mine, others)]
    return gaps[0] * gaps[0] + gaps[1] * gaps[1] + gaps[2] * gaps[2]


def early_kernel(dens_ref, pair_ref, emb_ref, mid_ref, sum_ref, coef_ref, source, turned):
    for k in range(4):
        coef_ref[k : k + 1] = jnp.full((1, SLOTS), dens_ref[k], jnp.float32)
        coef_ref[4 + k : 5 + k] = jnp.full((1, SLOTS), pair_ref[k], jnp.float32)
    for k in range(2):
        coef_ref[8 + k : 9 + k] = jnp.full((1, SLOTS), emb_ref[k], jnp.float32)
    boxes = []
    for x in range(6):
        boxes.append((mid_ref[0, x], mid_ref[2, x]))
        for v in range(3):
            for c in range(3):
                base = 24 * (3 * v + c) + 4 * x
                low = max(0, 1 - v)
                high = min(4, 5 - v)
                block = mid_ref[c, x, low + v - 1 : high + v - 1]
                row = lax.broadcasted_iota(jnp.int32, block.shape, 0).astype(jnp.float32)
                block = block + (x - 2.5, row + (low + v - 2.5), 0.0)[c]
                source[base + low : base + high] = block
                for edge in (0,) * low + (3,) * (4 - high):
                    source[base + edge : base + edge + 1] = jnp.full((1, SLOTS), FAR, jnp.float32)
    a = monic([jnp.full((8, SLOTS), dens_ref[k], jnp.float32) for k in range(4)])

    def rows_of(ref, u, v, c, m):
        start = 24 * (3 * (v + 1) + c) + 4 * (1 + u) + 8 * m
        return ref[start : start + 8]

    mine = [[rows_of(source, 0, 0, c, m) for c in range(3)] for m in range(2)]

    def step(d, ref, totals):
        same = jnp.where(d == 0, 100.0, 0.0)
        totals = list(totals)
        for u in (-1, 0, 1):
            for v in (-1, 0, 1):
                for m in range(2):
                    square = square_of(mine[m], [rows_of(ref, u, v, c, m) for c in range(3)])
                    if u == 0 and v == 0:
                        square = square + same
                    totals[m] = totals[m] + density_term(square, a)
        return tuple(totals)

    zero = jnp.zeros((8, SLOTS), jnp.float32)
    totals = offsets_loop(reach_of(boxes), source, turned, step, (zero, zero))
    for m in range(2):
        sum_ref[8 * m : 8 * m + 8] = totals[m]


def late_kernel(
    mid_ref, low_ref, high_ref, half_ref, slot_ref, sum_ref, coef_ref,
    vel_ref, frc_ref, str_ref,
    rims, rims_turned, edges, slopes, packs, packs_turned,
):
    f32 = jnp.float32

    def block_row(c, x, y):
        if y < 2:
            values = low_ref[c, x, y : y + 1]
        elif y < 6:
            values = mid_ref[c, x, y - 2 : y - 1]
        else:
            values = high_ref[c, x, y - 6 : y - 5]
        return values + (x - 2.5, y - 3.5, 0.0)[c]

    for v in range(3):
        for c in range(3):
            for x in range(6):
                for s in range(2):
                    row = 12 * (3 * v + c) + 2 * x + s
                    rims[row : row + 1] = block_row(c, x, (1, 6)[s] + v - 1)
    boxes = []
    for x in range(6):
        boxes.append((mid_ref[0, x], mid_ref[2, x]))
        boxes.append((low_ref[0, x], low_ref[2, x]))
        boxes.append((high_ref[0, x], high_ref[2, x]))
    reach = reach_of(boxes)

    def coef(k):
        return jnp.broadcast_to(coef_ref[k : k + 1], (8, SLOTS))

    a = [coef(k) for k in range(4)]
    p = [coef(4 + k) for k in range(4)]
    am = monic(a)

    def rim(ref, u, v, c):
        start = 12 * (3 * (v + 1) + c) + 2 * (1 + u)
        return ref[start : start + 8]

    outer = [rim(rims, 0, 0, c) for c in range(3)]
    for c in range(3):
        for x in range(4):
            for s in range(2):
                edges[c, 2 * x + s : 2 * x + s + 1] = block_row(c, x + 1, (2, 5)[s])
    inner = [edges[c] for c in range(3)]

    def density_step(d, ref, totals):
        same = jnp.where(d == 0, 100.0, 0.0)
        out, inn = totals
        for u in (-1, 0, 1):
            for v in (-1, 0, 1):
                others = [rim(ref, u, v, c) for c in range(3)]
                square = square_of(outer, others)
                if u == 0 and v == 0:
                    square = square + same
                out = out + density_term(square, am)
                if v == 0:
                    inn = inn + density_term(square_of(inner, others), am)
        return (out, inn)

    zero = jnp.zeros((8, SLOTS), f32)
    out, inn = offsets_loop(reach, rims, rims_turned, density_step, (zero, zero))
    edges[0] = out
    edges[1] = inn
    for x in range(4):
        for s in range(2):
            row = 2 * x + s
            slopes[6 * x + 5 * s : 6 * x + 5 * s + 1] = edges[0, row : row + 1]
            mine = 4 * x + 3 * s
            slopes[6 * x + 3 * s + 1 : 6 * x + 3 * s + 2] = (
                sum_ref[mine : mine + 1] + edges[1, row : row + 1]
            )
        slopes[6 * x + 2 : 6 * x + 4] = sum_ref[4 * x + 1 : 4 * x + 3]
    for m in range(3):
        total = slopes[8 * m : 8 * m + 8] * a[3]
        slope = (-0.5 * coef(8)) / jnp.sqrt(1.0 + total) + (2.0 * coef(9)) * total
        slopes[8 * m : 8 * m + 8] = slope * (a[3] / p[3])

    for u in (-1, 0, 1):
        for v in (-1, 0, 1):
            k = 3 * (u + 1) + v + 1
            for s in range(2):
                x = 2 + s + u
                for c in range(3):
                    base = 8 * (4 * k + c) + 4 * s
                    for y in range(2 + v, 6 + v):
                        if y in (1, 6):
                            packs[base + y - 2 - v : base + y - 1 - v] = block_row(c, x, y)
                    first = max(2, 2 + v)
                    last = min(6, 6 + v)
                    block = mid_ref[c, x, first - 2 : last - 2]
                    row = lax.broadcasted_iota(jnp.int32, block.shape, 0).astype(f32)
                    block = block + (x - 2.5, row + (first - 3.5), 0.0)[c]
                    packs[base + first - 2 - v : base + last - 2 - v] = block
                base = 8 * (4 * k + 3) + 4 * s
                start = 6 * (x - 1) + 1 + v
                packs[base : base + 4] = slopes[start : start + 4]

    def member(ref, k, c):
        return ref[8 * (4 * k + c) : 8 * (4 * k + c) + 8]

    own = [member(packs, 4, c) for c in range(4)]
    gd = monic([(k + 2.0) * a[k] for k in range(4)])
    gp = monic([(k + 2.0) * p[k] for k in range(4)])

    def force_step(d, ref, sums):
        same = jnp.where(d == 0, 100.0, 0.0)
        sums = list(sums)
        for k in range(9):
            gaps = [own[c] - member(ref, k, c) for c in range(3)]
            square = gaps[0] * gaps[0] + gaps[1] * gaps[1] + gaps[2] * gaps[2]
            if k == 4:
                square = square + same
            w = jnp.maximum(1.0 - square, 0.0)
            slope = own[3] + member(ref, k, 3)
            strength = w * (slope * cubic(w, gd) + cubic(w, gp))
            pulls = [strength * gap for gap in gaps]
            for c in range(3):
                sums[c] = sums[c] + pulls[c]
            for t, (r, s) in enumerate(stress_pairs):
                sums[3 + t] = sums[3 + t] + gaps[r] * pulls[s]
        return tuple(sums)

    sums = offsets_loop(reach, packs, packs_turned, force_step, (zero,) * 9)
    slot = slot_ref[...]
    alive = slot >= 0
    index = jnp.maximum(slot, 0)

    def restored(values, scale):
        moved = jnp.take_along_axis(values, index, axis=1)
        return jnp.where(alive, moved * (scale * p[3]), 0.0)

    for c in range(3):
        force = restored(sums[c], 10.0 / cutoff)
        frc_ref[c] = force
        vel_ref[c] = half_ref[c] + kick_scale * force
    for t in range(6):
        str_ref[t] = restored(sums[3 + t], 5.0 / atom_volume)


def shifted(block, axis, distance):
    count = lax.axis_size(axis)
    route = [(i, (i + distance) % count) for i in range(count)]
    return lax.ppermute(block, axis, route)


def body(position, velocity, force_old, counts, density_coef, pair_coef, embed_coef):
    shape = position.shape
    flat = (3, 8, SLOTS)
    vmem = pl.BlockSpec(memory_space=pltpu.VMEM)
    smem = pl.BlockSpec(memory_space=pltpu.SMEM)
    hbm = pl.BlockSpec(memory_space=pltpu.HBM)
    f32 = jnp.float32
    new, half, pay, slot = pl.pallas_call(
        place_kernel,
        in_specs=[hbm] * 4,
        out_specs=[vmem] * 4,
        out_shape=[jax.ShapeDtypeStruct(flat, f32)] * 3
        + [jax.ShapeDtypeStruct((8, SLOTS), jnp.int32)],
        scratch_shapes=[
            pltpu.VMEM((3,) + flat, f32),
            pltpu.SMEM(counts.shape, jnp.int32),
            pltpu.SemaphoreType.DMA((4,)),
        ],
        compiler_params=pltpu.CompilerParams(vmem_limit_bytes=GRANT),
        name="place",
    )(
        *[
            pltpu.with_memory_space_constraint(source, pltpu.HBM)
            for source in (
                counts,
                position.reshape(flat),
                velocity.reshape(flat),
                force_old.reshape(flat),
            )
        ],
    )
    pay = pay.reshape(shape)
    before = shifted(pay, "gx", 1)
    after = shifted(pay, "gx", -1)
    mid = jnp.concatenate([before, pay, after], axis=1)
    count = lax.axis_size("gy")
    even = lax.axis_index("gy") % 2 == 0
    swap = [(i, i + 1 - 2 * (i % 2)) for i in range(count)]
    mate = lax.ppermute(mid, "gy", swap)
    early = pl.pallas_call(
        early_kernel,
        in_specs=[smem] * 3 + [vmem],
        out_specs=[vmem] * 2,
        out_shape=[jax.ShapeDtypeStruct((16, SLOTS), f32)] * 2,
        scratch_shapes=[pltpu.VMEM((216, SLOTS), f32), pltpu.VMEM((2, 216, SLOTS), f32)],
        cost_estimate=pl.CostEstimate(flops=12000000, bytes_accessed=60000, transcendentals=0),
        compiler_params=pltpu.CompilerParams(vmem_limit_bytes=GRANT),
        name="early",
    )
    total, coefs = early(density_coef, pair_coef, embed_coef, mid)
    passed = jnp.where(even, mate[:, :, 2:], mate[:, :, :2])
    route = [(i, (i + 2 - 4 * (i % 2)) % count) for i in range(count)]
    far = lax.ppermute(passed, "gy", route)
    low = jnp.where(even, far, mate[:, :, 2:])
    high = jnp.where(even, mate[:, :, :2], far)
    vel, frc, stress = pl.pallas_call(
        late_kernel,
        in_specs=[vmem] * 7,
        out_specs=[vmem] * 3,
        out_shape=[
            jax.ShapeDtypeStruct(flat, f32),
            jax.ShapeDtypeStruct(flat, f32),
            jax.ShapeDtypeStruct((6, 8, SLOTS), f32),
        ],
        scratch_shapes=[
            pltpu.VMEM((112, SLOTS), f32),
            pltpu.VMEM((2, 112, SLOTS), f32),
            pltpu.VMEM((3, 8, SLOTS), f32),
            pltpu.VMEM((24, SLOTS), f32),
            pltpu.VMEM((288, SLOTS), f32),
            pltpu.VMEM((2, 288, SLOTS), f32),
        ],
        compiler_params=pltpu.CompilerParams(vmem_limit_bytes=GRANT),
        name="late",
    )(mid, low, high, half, slot, total, coefs)
    return (
        new.reshape(shape),
        vel.reshape(shape),
        frc.reshape(shape),
        stress.reshape((6,) + shape[1:]),
    )


def solution(mesh):
    grid = P(None, "gx", "gy", None)
    return jax.shard_map(
        body,
        mesh=mesh,
        in_specs=(grid, grid, grid, P("gx", "gy"), P(), P(), P()),
        out_specs=(grid, grid, grid, grid),
        check_vma=False,
    )
```

```python
import jax
import jax.numpy as jnp
from jax import lax
from jax.experimental import pallas as pl
from jax.experimental.pallas import tpu as pltpu
from jax.sharding import PartitionSpec as P


cutoff = 5.5
time_step = 0.004
inverse_mass = 151.83
atom_volume = 11.8
kick_scale = 0.5 * time_step * inverse_mass
stress_pairs = ((0, 0), (1, 1), (2, 2), (0, 1), (0, 2), (1, 2))
SLOTS = 128
SLOTS_PER_A = 128.0 / 48.0
SLOT_LEAD = 1.5
FAR = 1.0e4
NONE = -1.0e6
GRANT = 8 * 2**20
UNROLL = 8


def place_kernel(
    counts_hbm, pos_hbm, vel_hbm, frc_hbm,
    new_ref, half_ref, pay_ref, slot_ref,
    fetched, counts_ref, arrived,
):
    copies = [
        pltpu.make_async_copy(source, fetched.at[k], arrived.at[k])
        for k, source in enumerate((pos_hbm, vel_hbm, frc_hbm))
    ]
    copies.append(pltpu.make_async_copy(counts_hbm, counts_ref, arrived.at[3]))
    for copy in copies:
        copy.start()
    for copy in copies:
        copy.wait()
    pos_ref, vel_ref, frc_ref = [fetched.at[k] for k in range(3)]
    half = [vel_ref[c] + kick_scale * frc_ref[c] for c in range(3)]
    new = [pos_ref[c] + time_step * half[c] for c in range(3)]
    for c in range(3):
        half_ref[c] = half[c]
        new_ref[c] = new[c]
    rows = lax.broadcasted_iota(jnp.int32, (8, SLOTS), 0)
    lane_int = lax.broadcasted_iota(jnp.int32, (8, SLOTS), 1)
    lane = lane_int.astype(jnp.float32)
    count = jnp.zeros((8, SLOTS), jnp.int32)
    for b in range(8):
        count = jnp.where(rows == b, counts_ref[b // 4, b % 4], count)
    alive = lane_int < count
    wanted = new[2] * SLOTS_PER_A - SLOT_LEAD
    fine = jnp.clip(jnp.floor((wanted + 8.0) * 64.0), 0.0, 16383.0)
    key = jnp.where(alive, fine, 32768.0) * 128.0 + lane
    wanted = jnp.clip(jnp.floor(wanted), 0.0, 127.0)

    def column(values_t, b):
        return jnp.broadcast_to(values_t[:, b : b + 1], (SLOTS, SLOTS))

    key_t = key.T
    ranks = []
    for b in range(8):
        before = column(key_t, b) < key[b : b + 1]
        ranks.append(jnp.sum(jnp.where(before, 1.0, 0.0), axis=0, keepdims=True))
    rank = jnp.concatenate(ranks, axis=0)
    lead = jnp.where(alive, wanted - rank, NONE)
    lead_t = lead.T
    leads = []
    for b in range(8):
        before = column(key_t, b) < key[b : b + 1]
        leads.append(jnp.max(jnp.where(before, column(lead_t, b), NONE), axis=0, keepdims=True))
    slot = rank + jnp.maximum(lead, jnp.concatenate(leads, axis=0))
    slot = jnp.minimum(slot, 128.0 - count.astype(jnp.float32) + rank)
    slot = jnp.where(alive, slot, -1.0)
    slot_ref[...] = slot.astype(jnp.int32)
    slot_t = slot.T
    atom = lax.broadcasted_iota(jnp.int32, (SLOTS, SLOTS), 0).astype(jnp.float32)
    lanes = lax.broadcasted_iota(jnp.int32, (SLOTS, SLOTS), 1).astype(jnp.float32)
    owners = []
    for b in range(8):
        owners.append(
            jnp.max(jnp.where(column(slot_t, b) == lanes, atom, -1.0), axis=0, keepdims=True)
        )
    owner = jnp.concatenate(owners, axis=0)
    taken = owner >= 0.0
    index = jnp.maximum(owner, 0.0).astype(jnp.int32)
    for c in range(3):
        moved = jnp.take_along_axis(new[c], index, axis=1) * (1.0 / cutoff)
        pay_ref[c] = jnp.where(taken, moved, FAR if c == 0 else 0.0)


def gap_range(boxes):
    most, least = (None, None)
    for far, height in boxes:
        lane = lax.broadcasted_iota(jnp.int32, height.shape, 1).astype(jnp.float32)
        gap = lane - height * (cutoff * SLOTS_PER_A)
        there = far < 100.0
        high = jnp.where(there, gap, -1.0e6)
        low = jnp.where(there, gap, 1.0e6)
        most = high if most is None else jnp.maximum(most, high)
        least = low if least is None else jnp.minimum(least, low)
    return jnp.max(most, axis=0, keepdims=True), jnp.min(least, axis=0, keepdims=True)


def reach_of(most, least):
    reach = jnp.max(most) - jnp.min(least) + (cutoff * SLOTS_PER_A + 0.01)
    return jnp.clip(reach, 0.0, 64.0).astype(jnp.int32)


def joined(one, two):
    return jnp.maximum(one[0], two[0]), jnp.minimum(one[1], two[1])


def offsets_loop(reach, source, turned, step, start):
    rows = source.shape[0]

    def turn(d, ref):
        by = lax.bitwise_and(-d, SLOTS - 1)
        for r in range(0, rows, 8):
            ref[r : r + 8] = pltpu.roll(source[r : r + 8], by, 1)

    def several(i, carry):
        for k in range(UNROLL):
            d = UNROLL * i + k - reach
            turn(d + 1, turned.at[1 - k % 2])
            carry = step(d, turned.at[k % 2], carry)
        return carry

    turn(-reach, turned.at[0])
    trips = (2 * reach + UNROLL) // UNROLL
    return lax.fori_loop(0, jnp.minimum(trips, SLOTS // UNROLL), several, start)


def monic(coefs):
    return [c / coefs[3] for c in coefs[:3]]


def cubic(w, m):
    return m[0] + w * (m[1] + w * (m[2] + w))


def density_term(square, m):
    w = jnp.maximum(1.0 - square, 0.0)
    return (w * w) * cubic(w, m)


def square_of(mine, others):
    gaps = [m - o for m, o in zip(mine, others)]
    return gaps[0] * gaps[0] + gaps[1] * gaps[1] + gaps[2] * gaps[2]


def early_kernel(
    dens_ref, pair_ref, emb_ref, mid_ref, sum_ref, coef_ref, range_ref, source, turned
):
    for k in range(4):
        coef_ref[k : k + 1] = jnp.full((1, SLOTS), dens_ref[k], jnp.float32)
        coef_ref[4 + k : 5 + k] = jnp.full((1, SLOTS), pair_ref[k], jnp.float32)
    for k in range(2):
        coef_ref[8 + k : 9 + k] = jnp.full((1, SLOTS), emb_ref[k], jnp.float32)
    boxes = []
    for x in range(6):
        boxes.append((mid_ref[0, x], mid_ref[2, x]))
        for v in range(3):
            for c in range(3):
                base = 24 * (3 * v + c) + 4 * x
                low = max(0, 1 - v)
                high = min(4, 5 - v)
                block = mid_ref[c, x, low + v - 1 : high + v - 1]
                row = lax.broadcasted_iota(jnp.int32, block.shape, 0).astype(jnp.float32)
                block = block + (x - 2.5, row + (low + v - 2.5), 0.0)[c]
                source[base + low : base + high] = block
                for edge in (0,) * low + (3,) * (4 - high):
                    source[base + edge : base + edge + 1] = jnp.full((1, SLOTS), FAR, jnp.float32)
    a = monic([jnp.full((8, SLOTS), dens_ref[k], jnp.float32) for k in range(4)])

    def rows_of(ref, u, v, c, m):
        start = 24 * (3 * (v + 1) + c) + 4 * (1 + u) + 8 * m
        return ref[start : start + 8]

    mine = [[rows_of(source, 0, 0, c, m) for c in range(3)] for m in range(2)]

    def step(d, ref, totals):
        same = jnp.where(d == 0, 100.0, 0.0)
        totals = list(totals)
        for u in (-1, 0, 1):
            for v in (-1, 0, 1):
                for m in range(2):
                    square = square_of(mine[m], [rows_of(ref, u, v, c, m) for c in range(3)])
                    if u == 0 and v == 0:
                        square = square + same
                    totals[m] = totals[m] + density_term(square, a)
        return tuple(totals)

    zero = jnp.zeros((8, SLOTS), jnp.float32)
    extent = gap_range(boxes)
    for k in range(2):
        range_ref[k : k + 1] = extent[k]
    totals = offsets_loop(reach_of(*extent), source, turned, step, (zero, zero))
    for m in range(2):
        sum_ref[8 * m : 8 * m + 8] = totals[m]


def rim_density(high, mid_ref, halo_ref, rows, a, extent, source, turned, sides, out_ref):
    sign = (2 * high - 1).astype(jnp.float32)

    def depth_row(c, x, t):
        if t == 0:
            values = mid_ref[c, x, pl.ds(3 * high, 1)]
        else:
            values = halo_ref[c, x, pl.ds(rows[t - 1], 1)]
        if c == 1:
            return values + sign * (1.5 + t)
        return values + (x - 2.5) if c == 0 else values

    for c in range(3):
        for x in range(6):
            base = 24 * c + 2 * x
            source[base : base + 1] = depth_row(c, x, 0)
            source[base + 1 : base + 2] = depth_row(c, x, 2)
            near = depth_row(c, x, 1)
            source[base + 12 : base + 13] = near
            source[base + 13 : base + 14] = near
            if 1 <= x <= 4:
                row = 2 * (x - 1)
                sides[0, c, row : row + 1] = near
                sides[0, c, row + 1 : row + 2] = near
                sides[1, c, row : row + 1] = near
                sides[1, c, row + 1 : row + 2] = depth_row(c, x, 0)
    mine = [[sides[k, c] for c in range(3)] for k in range(2)]
    row_at = lax.broadcasted_iota(jnp.int32, (8, SLOTS), 0)
    itself = jnp.where(lax.bitwise_and(row_at, 1) == 0, 100.0, 0.0)

    def step(d, ref, totals):
        same = jnp.where(d == 0, 1.0, 0.0)
        totals = list(totals)
        for u in (-1, 0, 1):
            for k in range(2):
                starts = [24 * c + 12 * k + 2 * (1 + u) for c in range(3)]
                square = square_of(mine[k], [ref[r : r + 8] for r in starts])
                if u == 0 and k == 1:
                    square = square + itself * same
                totals[k] = totals[k] + density_term(square, a)
        return tuple(totals)

    zero = jnp.zeros((8, SLOTS), jnp.float32)
    totals = offsets_loop(reach_of(*extent), source, turned, step, (zero, zero))
    for k in range(2):
        sides[k, 0] = totals[k]
    for x in range(4):
        row = 2 * x
        out_ref[x : x + 1] = (
            sides[0, 0, row : row + 1] + sides[0, 0, row + 1 : row + 2] + sides[1, 0, row : row + 1]
        )
        out_ref[4 + x : 5 + x] = sides[1, 0, row + 1 : row + 2]


def side_of_mate():
    return 1 - lax.rem(lax.axis_index("gy"), 2)


def mate_kernel(mid_ref, mate_ref, coef_ref, range_ref, sum_ref, wide_ref, source, turned, sides):
    high = side_of_mate()
    boxes = [
        (mate_ref[0, x, pl.ds(2 - 2 * high, 2)], mate_ref[2, x, pl.ds(2 - 2 * high, 2)])
        for x in range(6)
    ]
    extent = joined(gap_range(boxes), (range_ref[0:1], range_ref[1:2]))
    for k in range(2):
        wide_ref[k : k + 1] = extent[k]
    a = monic([jnp.broadcast_to(coef_ref[k : k + 1], (8, SLOTS)) for k in range(4)])
    rows = (3 - 3 * high, 2 - high)
    rim_density(high, mid_ref, mate_ref, rows, a, extent, source, turned, sides, sum_ref)


def late_kernel(
    mid_ref, mate_ref, far_ref, half_ref, slot_ref, sum_ref, rim_ref, coef_ref, range_ref,
    vel_ref, frc_ref, str_ref,
    source, turned, sides, far_rim, slopes, packs, packs_turned,
):
    f32 = jnp.float32
    mate_high = side_of_mate()
    far_high = 1 - mate_high

    def coef(k):
        return jnp.broadcast_to(coef_ref[k : k + 1], (8, SLOTS))

    a = [coef(k) for k in range(4)]
    p = [coef(4 + k) for k in range(4)]
    am = monic(a)
    zero = jnp.zeros((8, SLOTS), f32)
    boxes = [(far_ref[0, x], far_ref[2, x]) for x in range(6)]
    extent = joined(gap_range(boxes), (range_ref[0:1], range_ref[1:2]))
    reach = reach_of(*extent)
    far_rows = (1 - far_high, far_high)
    rim_density(far_high, mid_ref, far_ref, far_rows, am, extent, source, turned, sides, far_rim)
    for x in range(4):
        slopes[6 * x + 2 : 6 * x + 4] = sum_ref[4 * x + 1 : 4 * x + 3]
        for high, rim in ((mate_high, rim_ref), (far_high, far_rim)):
            slopes[pl.ds(6 * x + 5 * high, 1)] = rim[x : x + 1]
            slopes[pl.ds(6 * x + 1 + 3 * high, 1)] = (
                sum_ref[pl.ds(4 * x + 3 * high, 1)] + rim[4 + x : 5 + x]
            )
    for m in range(3):
        total = slopes[8 * m : 8 * m + 8] * a[3]
        slope = (-0.5 * coef(8)) / jnp.sqrt(1.0 + total) + (2.0 * coef(9)) * total
        slopes[8 * m : 8 * m + 8] = slope * (a[3] / p[3])

    for high, halo, near in (
        (mate_high, mate_ref, 3 - 3 * mate_high),
        (far_high, far_ref, far_rows[0]),
    ):
        height = (2 * high - 1).astype(f32) * 2.5
        for u in (-1, 0, 1):
            for s in range(2):
                x = 2 + s + u
                for c in range(3):
                    values = halo[c, x, pl.ds(near, 1)] + (x - 2.5, height, 0.0)[c]
                    packs[pl.ds(96 * (u + 1) + 8 * c + 4 * s + 67 * high, 1)] = values
    for u in (-1, 0, 1):
        for v in (-1, 0, 1):
            k = 3 * (u + 1) + v + 1
            for s in range(2):
                x = 2 + s + u
                for c in range(3):
                    base = 8 * (4 * k + c) + 4 * s
                    first = max(2, 2 + v)
                    last = min(6, 6 + v)
                    block = mid_ref[c, x, first - 2 : last - 2]
                    row = lax.broadcasted_iota(jnp.int32, block.shape, 0).astype(f32)
                    block = block + (x - 2.5, row + (first - 3.5), 0.0)[c]
                    packs[base + first - 2 - v : base + last - 2 - v] = block
                base = 8 * (4 * k + 3) + 4 * s
                start = 6 * (x - 1) + 1 + v
                packs[base : base + 4] = slopes[start : start + 4]

    def member(ref, k, c):
        return ref[8 * (4 * k + c) : 8 * (4 * k + c) + 8]

    own = [member(packs, 4, c) for c in range(4)]
    gd = monic([(k + 2.0) * a[k] for k in range(4)])
    gp = monic([(k + 2.0) * p[k] for k in range(4)])

    def force_step(d, ref, sums):
        same = jnp.where(d == 0, 100.0, 0.0)
        sums = list(sums)
        for k in range(9):
            gaps = [own[c] - member(ref, k, c) for c in range(3)]
            square = gaps[0] * gaps[0] + gaps[1] * gaps[1] + gaps[2] * gaps[2]
            if k == 4:
                square = square + same
            w = jnp.maximum(1.0 - square, 0.0)
            slope = own[3] + member(ref, k, 3)
            strength = w * (slope * cubic(w, gd) + cubic(w, gp))
            pulls = [strength * gap for gap in gaps]
            for c in range(3):
                sums[c] = sums[c] + pulls[c]
            for t, (r, s) in enumerate(stress_pairs):
                sums[3 + t] = sums[3 + t] + gaps[r] * pulls[s]
        return tuple(sums)

    sums = offsets_loop(reach, packs, packs_turned, force_step, (zero,) * 9)
    slot = slot_ref[...]
    alive = slot >= 0
    index = jnp.maximum(slot, 0)

    def restored(values, scale):
        moved = jnp.take_along_axis(values, index, axis=1)
        return jnp.where(alive, moved * (scale * p[3]), 0.0)

    for c in range(3):
        force = restored(sums[c], 10.0 / cutoff)
        frc_ref[c] = force
        vel_ref[c] = half_ref[c] + kick_scale * force
    for t in range(6):
        str_ref[t] = restored(sums[3 + t], 5.0 / atom_volume)


def shifted(block, axis, distance):
    count = lax.axis_size(axis)
    route = [(i, (i + distance) % count) for i in range(count)]
    return lax.ppermute(block, axis, route)


def body(position, velocity, force_old, counts, density_coef, pair_coef, embed_coef):
    shape = position.shape
    flat = (3, 8, SLOTS)
    vmem = pl.BlockSpec(memory_space=pltpu.VMEM)
    smem = pl.BlockSpec(memory_space=pltpu.SMEM)
    hbm = pl.BlockSpec(memory_space=pltpu.HBM)
    f32 = jnp.float32
    new, half, pay, slot = pl.pallas_call(
        place_kernel,
        in_specs=[hbm] * 4,
        out_specs=[vmem] * 4,
        out_shape=[jax.ShapeDtypeStruct(flat, f32)] * 3
        + [jax.ShapeDtypeStruct((8, SLOTS), jnp.int32)],
        scratch_shapes=[
            pltpu.VMEM((3,) + flat, f32),
            pltpu.SMEM(counts.shape, jnp.int32),
            pltpu.SemaphoreType.DMA((4,)),
        ],
        compiler_params=pltpu.CompilerParams(vmem_limit_bytes=GRANT),
        name="place",
    )(
        *[
            pltpu.with_memory_space_constraint(source, pltpu.HBM)
            for source in (
                counts,
                position.reshape(flat),
                velocity.reshape(flat),
                force_old.reshape(flat),
            )
        ],
    )
    pay = pay.reshape(shape)
    before = shifted(pay, "gx", 1)
    after = shifted(pay, "gx", -1)
    mid = jnp.concatenate([before, pay, after], axis=1)
    count = lax.axis_size("gy")
    even = lax.axis_index("gy") % 2 == 0
    swap = [(i, i + 1 - 2 * (i % 2)) for i in range(count)]
    mate = lax.ppermute(mid, "gy", swap)
    early = pl.pallas_call(
        early_kernel,
        in_specs=[smem] * 3 + [vmem],
        out_specs=[vmem] * 3,
        out_shape=[jax.ShapeDtypeStruct((r, SLOTS), f32) for r in (16, 16, 8)],
        scratch_shapes=[pltpu.VMEM((216, SLOTS), f32), pltpu.VMEM((2, 216, SLOTS), f32)],
        cost_estimate=pl.CostEstimate(flops=12000000, bytes_accessed=60000, transcendentals=0),
        compiler_params=pltpu.CompilerParams(vmem_limit_bytes=GRANT),
        name="early",
    )
    total, coefs, extent = early(density_coef, pair_coef, embed_coef, mid)
    passed = jnp.where(even, mate[:, :, 2:], mate[:, :, :2])
    route = [(i, (i + 2 - 4 * (i % 2)) % count) for i in range(count)]
    far = lax.ppermute(passed, "gy", route)
    rim_scratch = [
        pltpu.VMEM((72, SLOTS), f32),
        pltpu.VMEM((2, 72, SLOTS), f32),
        pltpu.VMEM((2, 3, 8, SLOTS), f32),
    ]
    past_mate = pl.pallas_call(
        mate_kernel,
        in_specs=[vmem] * 4,
        out_specs=[vmem] * 2,
        out_shape=[jax.ShapeDtypeStruct((8, SLOTS), f32)] * 2,
        scratch_shapes=rim_scratch,
        cost_estimate=pl.CostEstimate(flops=5000000, bytes_accessed=60000, transcendentals=0),
        compiler_params=pltpu.CompilerParams(vmem_limit_bytes=GRANT),
        name="past_mate",
    )
    rim, wide = past_mate(mid, mate, coefs, extent)
    vel, frc, stress = pl.pallas_call(
        late_kernel,
        in_specs=[vmem] * 9,
        out_specs=[vmem] * 3,
        out_shape=[
            jax.ShapeDtypeStruct(flat, f32),
            jax.ShapeDtypeStruct(flat, f32),
            jax.ShapeDtypeStruct((6, 8, SLOTS), f32),
        ],
        scratch_shapes=rim_scratch
        + [
            pltpu.VMEM((8, SLOTS), f32),
            pltpu.VMEM((24, SLOTS), f32),
            pltpu.VMEM((288, SLOTS), f32),
            pltpu.VMEM((2, 288, SLOTS), f32),
        ],
        compiler_params=pltpu.CompilerParams(vmem_limit_bytes=GRANT),
        name="late",
    )(mid, mate, far, half, slot, total, rim, coefs, wide)
    return (
        new.reshape(shape),
        vel.reshape(shape),
        frc.reshape(shape),
        stress.reshape((6,) + shape[1:]),
    )


def solution(mesh):
    grid = P(None, "gx", "gy", None)
    return jax.shard_map(
        body,
        mesh=mesh,
        in_specs=(grid, grid, grid, P("gx", "gy"), P(), P(), P()),
        out_specs=(grid, grid, grid, grid),
        check_vma=False,
    )
```

```python
import jax
import jax.numpy as jnp
from jax import lax
from jax.experimental import pallas as pl
from jax.experimental.pallas import tpu as pltpu
from jax.sharding import PartitionSpec as P


cutoff = 5.5
time_step = 0.004
inverse_mass = 151.83
atom_volume = 11.8
kick_scale = 0.5 * time_step * inverse_mass
stress_pairs = ((0, 0), (1, 1), (2, 2), (0, 1), (0, 2), (1, 2))
SLOTS = 128
SLOTS_PER_A = 128.0 / 48.0
SLOT_LEAD = 1.5
FAR = 1.0e4
NONE = -256.0
GRANT = 8 * 2**20
UNROLL = 8


def place_kernel(
    counts_hbm, pos_hbm, vel_hbm, frc_hbm,
    new_ref, half_ref, pay_ref, slot_ref,
    fetched, counts_ref, arrived,
):
    copies = [
        pltpu.make_async_copy(source, fetched.at[k], arrived.at[k])
        for k, source in enumerate((pos_hbm, vel_hbm, frc_hbm))
    ]
    copies.append(pltpu.make_async_copy(counts_hbm, counts_ref, arrived.at[3]))
    for copy in copies:
        copy.start()
    row_at = lax.broadcasted_iota(jnp.int32, (24, 8 * SLOTS), 0)
    block_at = lax.shift_right_logical(lax.broadcasted_iota(jnp.int32, (24, 8 * SLOTS), 1), 7)
    weight = jnp.where(row_at < 8, 65536.0, jnp.where(row_at < 16, 256.0, 1.0))
    spread = jnp.where(lax.bitwise_and(row_at, 7) == block_at, weight, 0.0).astype(jnp.bfloat16)
    for copy in copies:
        copy.wait()
    pos_ref, vel_ref, frc_ref = [fetched.at[k] for k in range(3)]
    half = [vel_ref[c] + kick_scale * frc_ref[c] for c in range(3)]
    new = [pos_ref[c] + time_step * half[c] for c in range(3)]
    for c in range(3):
        half_ref[c] = half[c]
        new_ref[c] = new[c]
    rows = lax.broadcasted_iota(jnp.int32, (8, SLOTS), 0)
    lane_int = lax.broadcasted_iota(jnp.int32, (8, SLOTS), 1)
    lane = lane_int.astype(jnp.float32)
    count = jnp.zeros((8, SLOTS), jnp.int32)
    for b in range(8):
        count = jnp.where(rows == b, counts_ref[b // 4, b % 4], count)
    alive = lane_int < count
    wanted = new[2] * SLOTS_PER_A - SLOT_LEAD
    fine = jnp.clip(jnp.floor((wanted + 8.0) * 64.0), 0.0, 16383.0)
    key = jnp.where(alive, fine, 32768.0) * 128.0 + lane
    wanted = jnp.clip(jnp.floor(wanted), 0.0, 127.0)

    def columns(parts):
        parts_t = jnp.concatenate(parts, axis=0).T.astype(jnp.bfloat16)
        weights = spread[24 - 8 * len(parts) :]
        return jnp.dot(parts_t, weights, preferred_element_type=jnp.float32)

    def part(values, b):
        return values[:, SLOTS * b : SLOTS * (b + 1)]

    high = jnp.floor(key * (1.0 / 65536.0))
    middle = jnp.floor(key * (1.0 / 256.0))
    keys = columns([high, middle - 256.0 * high, key - 256.0 * middle])
    ranks = []
    for b in range(8):
        before = part(keys, b) < key[b : b + 1]
        ranks.append(jnp.sum(jnp.where(before, 1.0, 0.0), axis=0, keepdims=True))
    rank = jnp.concatenate(ranks, axis=0)
    lead = jnp.where(alive, wanted - rank, NONE)
    lead_columns = columns([lead])
    leads = []
    for b in range(8):
        before = part(keys, b) < key[b : b + 1]
        leads.append(
            jnp.max(jnp.where(before, part(lead_columns, b), NONE), axis=0, keepdims=True)
        )
    slot = rank + jnp.maximum(lead, jnp.concatenate(leads, axis=0))
    slot = jnp.minimum(slot, 128.0 - count.astype(jnp.float32) + rank)
    slot = jnp.where(alive, slot, -1.0)
    slot_ref[...] = slot.astype(jnp.int32)
    slot_columns = columns([slot])
    atom = lax.broadcasted_iota(jnp.int32, (SLOTS, SLOTS), 0).astype(jnp.float32)
    lanes = lax.broadcasted_iota(jnp.int32, (SLOTS, SLOTS), 1).astype(jnp.float32)
    owners = []
    for b in range(8):
        owners.append(
            jnp.max(jnp.where(part(slot_columns, b) == lanes, atom, -1.0), axis=0, keepdims=True)
        )
    owner = jnp.concatenate(owners, axis=0)
    taken = owner >= 0.0
    index = jnp.maximum(owner, 0.0).astype(jnp.int32)
    for c in range(3):
        moved = jnp.take_along_axis(new[c], index, axis=1) * (1.0 / cutoff)
        pay_ref[c] = jnp.where(taken, moved, FAR if c == 0 else 0.0)


def gap_range(boxes):
    most, least = (None, None)
    for far, height in boxes:
        lane = lax.broadcasted_iota(jnp.int32, height.shape, 1).astype(jnp.float32)
        gap = lane - height * (cutoff * SLOTS_PER_A)
        there = far < 100.0
        high = jnp.where(there, gap, -1.0e6)
        low = jnp.where(there, gap, 1.0e6)
        most = high if most is None else jnp.maximum(most, high)
        least = low if least is None else jnp.minimum(least, low)
    return jnp.max(most, axis=0, keepdims=True), jnp.min(least, axis=0, keepdims=True)


def reach_of(most, least):
    reach = jnp.max(most) - jnp.min(least) + (cutoff * SLOTS_PER_A + 0.01)
    return jnp.clip(reach, 0.0, 64.0).astype(jnp.int32)


def joined(one, two):
    return jnp.maximum(one[0], two[0]), jnp.minimum(one[1], two[1])


def offsets_loop(reach, source, turned, step, start):
    rows = source.shape[0]

    def turn(d, ref):
        by = lax.bitwise_and(-d, SLOTS - 1)
        for r in range(0, rows, 8):
            ref[r : r + 8] = pltpu.roll(source[r : r + 8], by, 1)

    def several(i, carry):
        for k in range(UNROLL):
            d = UNROLL * i + k - reach
            turn(d + 1, turned.at[1 - k % 2])
            carry = step(d, turned.at[k % 2], carry)
        return carry

    turn(-reach, turned.at[0])
    trips = (2 * reach + UNROLL) // UNROLL
    return lax.fori_loop(0, jnp.minimum(trips, SLOTS // UNROLL), several, start)


def monic(coefs):
    return [c / coefs[3] for c in coefs[:3]]


def cubic(w, m):
    return m[0] + w * (m[1] + w * (m[2] + w))


def density_term(square, m):
    w = jnp.maximum(1.0 - square, 0.0)
    return (w * w) * cubic(w, m)


def square_of(mine, others):
    gaps = [m - o for m, o in zip(mine, others)]
    return gaps[0] * gaps[0] + gaps[1] * gaps[1] + gaps[2] * gaps[2]


def early_kernel(
    dens_ref, pair_ref, emb_ref, mid_ref, new_ref,
    sum_ref, coef_ref, range_ref, out_ref,
    source, turned,
):
    out_ref[...] = new_ref[...]
    for k in range(4):
        coef_ref[k : k + 1] = jnp.full((1, SLOTS), dens_ref[k], jnp.float32)
        coef_ref[4 + k : 5 + k] = jnp.full((1, SLOTS), pair_ref[k], jnp.float32)
    for k in range(2):
        coef_ref[8 + k : 9 + k] = jnp.full((1, SLOTS), emb_ref[k], jnp.float32)
    boxes = []
    for x in range(6):
        boxes.append((mid_ref[0, x], mid_ref[2, x]))
        for v in range(3):
            for c in range(3):
                base = 24 * (3 * v + c) + 4 * x
                low = max(0, 1 - v)
                high = min(4, 5 - v)
                block = mid_ref[c, x, low + v - 1 : high + v - 1]
                row = lax.broadcasted_iota(jnp.int32, block.shape, 0).astype(jnp.float32)
                block = block + (x - 2.5, row + (low + v - 2.5), 0.0)[c]
                source[base + low : base + high] = block
                for edge in (0,) * low + (3,) * (4 - high):
                    source[base + edge : base + edge + 1] = jnp.full((1, SLOTS), FAR, jnp.float32)
    a = monic([jnp.full((8, SLOTS), dens_ref[k], jnp.float32) for k in range(4)])

    def rows_of(ref, u, v, c, m):
        start = 24 * (3 * (v + 1) + c) + 4 * (1 + u) + 8 * m
        return ref[start : start + 8]

    mine = [[rows_of(source, 0, 0, c, m) for c in range(3)] for m in range(2)]

    def step(d, ref, totals):
        same = jnp.where(d == 0, 100.0, 0.0)
        totals = list(totals)
        for u in (-1, 0, 1):
            for v in (-1, 0, 1):
                for m in range(2):
                    square = square_of(mine[m], [rows_of(ref, u, v, c, m) for c in range(3)])
                    if u == 0 and v == 0:
                        square = square + same
                    totals[m] = totals[m] + density_term(square, a)
        return tuple(totals)

    zero = jnp.zeros((8, SLOTS), jnp.float32)
    extent = gap_range(boxes)
    for k in range(2):
        range_ref[k : k + 1] = extent[k]
    totals = offsets_loop(reach_of(*extent), source, turned, step, (zero, zero))
    for m in range(2):
        sum_ref[8 * m : 8 * m + 8] = totals[m]


def rim_density(high, mid_ref, halo_ref, rows, a, extent, source, turned, sides, out_ref):
    sign = (2 * high - 1).astype(jnp.float32)

    def depth_row(c, x, t):
        if t == 0:
            values = mid_ref[c, x, pl.ds(3 * high, 1)]
        else:
            values = halo_ref[c, x, pl.ds(rows[t - 1], 1)]
        if c == 1:
            return values + sign * (1.5 + t)
        return values + (x - 2.5) if c == 0 else values

    for c in range(3):
        for x in range(6):
            base = 24 * c + 2 * x
            source[base : base + 1] = depth_row(c, x, 0)
            source[base + 1 : base + 2] = depth_row(c, x, 2)
            near = depth_row(c, x, 1)
            source[base + 12 : base + 13] = near
            source[base + 13 : base + 14] = near
            if 1 <= x <= 4:
                row = 2 * (x - 1)
                sides[0, c, row : row + 1] = near
                sides[0, c, row + 1 : row + 2] = near
                sides[1, c, row : row + 1] = near
                sides[1, c, row + 1 : row + 2] = depth_row(c, x, 0)
    mine = [[sides[k, c] for c in range(3)] for k in range(2)]
    row_at = lax.broadcasted_iota(jnp.int32, (8, SLOTS), 0)
    itself = jnp.where(lax.bitwise_and(row_at, 1) == 0, 100.0, 0.0)

    def step(d, ref, totals):
        same = jnp.where(d == 0, 1.0, 0.0)
        totals = list(totals)
        for u in (-1, 0, 1):
            for k in range(2):
                starts = [24 * c + 12 * k + 2 * (1 + u) for c in range(3)]
                square = square_of(mine[k], [ref[r : r + 8] for r in starts])
                if u == 0 and k == 1:
                    square = square + itself * same
                totals[k] = totals[k] + density_term(square, a)
        return tuple(totals)

    zero = jnp.zeros((8, SLOTS), jnp.float32)
    totals = offsets_loop(reach_of(*extent), source, turned, step, (zero, zero))
    for k in range(2):
        sides[k, 0] = totals[k]
    for x in range(4):
        row = 2 * x
        out_ref[x : x + 1] = (
            sides[0, 0, row : row + 1] + sides[0, 0, row + 1 : row + 2] + sides[1, 0, row : row + 1]
        )
        out_ref[4 + x : 5 + x] = sides[1, 0, row + 1 : row + 2]


def side_of_mate():
    return 1 - lax.rem(lax.axis_index("gy"), 2)


def mate_kernel(mid_ref, mate_ref, coef_ref, range_ref, sum_ref, wide_ref, source, turned, sides):
    high = side_of_mate()
    boxes = [
        (mate_ref[0, x, pl.ds(2 - 2 * high, 2)], mate_ref[2, x, pl.ds(2 - 2 * high, 2)])
        for x in range(6)
    ]
    extent = joined(gap_range(boxes), (range_ref[0:1], range_ref[1:2]))
    for k in range(2):
        wide_ref[k : k + 1] = extent[k]
    a = monic([jnp.broadcast_to(coef_ref[k : k + 1], (8, SLOTS)) for k in range(4)])
    rows = (3 - 3 * high, 2 - high)
    rim_density(high, mid_ref, mate_ref, rows, a, extent, source, turned, sides, sum_ref)


def late_kernel(
    mid_ref, mate_ref, far_ref, half_ref, slot_ref, sum_ref, rim_ref, coef_ref, range_ref,
    vel_ref, frc_ref, str_ref,
    source, turned, sides, far_rim, slopes, packs, packs_turned,
):
    f32 = jnp.float32
    mate_high = side_of_mate()
    far_high = 1 - mate_high

    def coef(k):
        return jnp.broadcast_to(coef_ref[k : k + 1], (8, SLOTS))

    a = [coef(k) for k in range(4)]
    p = [coef(4 + k) for k in range(4)]
    am = monic(a)
    zero = jnp.zeros((8, SLOTS), f32)
    boxes = [(far_ref[0, x], far_ref[2, x]) for x in range(6)]
    extent = joined(gap_range(boxes), (range_ref[0:1], range_ref[1:2]))
    reach = reach_of(*extent)
    far_rows = (1 - far_high, far_high)
    rim_density(far_high, mid_ref, far_ref, far_rows, am, extent, source, turned, sides, far_rim)
    for x in range(4):
        slopes[6 * x + 2 : 6 * x + 4] = sum_ref[4 * x + 1 : 4 * x + 3]
        for high, rim in ((mate_high, rim_ref), (far_high, far_rim)):
            slopes[pl.ds(6 * x + 5 * high, 1)] = rim[x : x + 1]
            slopes[pl.ds(6 * x + 1 + 3 * high, 1)] = (
                sum_ref[pl.ds(4 * x + 3 * high, 1)] + rim[4 + x : 5 + x]
            )
    for m in range(3):
        total = slopes[8 * m : 8 * m + 8] * a[3]
        slope = (-0.5 * coef(8)) / jnp.sqrt(1.0 + total) + (2.0 * coef(9)) * total
        slopes[8 * m : 8 * m + 8] = slope * (a[3] / p[3])

    for high, halo, near in (
        (mate_high, mate_ref, 3 - 3 * mate_high),
        (far_high, far_ref, far_rows[0]),
    ):
        height = (2 * high - 1).astype(f32) * 2.5
        for u in (-1, 0, 1):
            for s in range(2):
                x = 2 + s + u
                for c in range(3):
                    values = halo[c, x, pl.ds(near, 1)] + (x - 2.5, height, 0.0)[c]
                    packs[pl.ds(96 * (u + 1) + 8 * c + 4 * s + 67 * high, 1)] = values
    for u in (-1, 0, 1):
        for v in (-1, 0, 1):
            k = 3 * (u + 1) + v + 1
            for s in range(2):
                x = 2 + s + u
                for c in range(3):
                    base = 8 * (4 * k + c) + 4 * s
                    first = max(2, 2 + v)
                    last = min(6, 6 + v)
                    block = mid_ref[c, x, first - 2 : last - 2]
                    row = lax.broadcasted_iota(jnp.int32, block.shape, 0).astype(f32)
                    block = block + (x - 2.5, row + (first - 3.5), 0.0)[c]
                    packs[base + first - 2 - v : base + last - 2 - v] = block
                base = 8 * (4 * k + 3) + 4 * s
                start = 6 * (x - 1) + 1 + v
                packs[base : base + 4] = slopes[start : start + 4]

    def member(ref, k, c):
        return ref[8 * (4 * k + c) : 8 * (4 * k + c) + 8]

    own = [member(packs, 4, c) for c in range(4)]
    gd = monic([(k + 2.0) * a[k] for k in range(4)])
    gp = monic([(k + 2.0) * p[k] for k in range(4)])

    def force_step(d, ref, sums):
        same = jnp.where(d == 0, 100.0, 0.0)
        sums = list(sums)
        for k in range(9):
            gaps = [own[c] - member(ref, k, c) for c in range(3)]
            square = gaps[0] * gaps[0] + gaps[1] * gaps[1] + gaps[2] * gaps[2]
            if k == 4:
                square = square + same
            w = jnp.maximum(1.0 - square, 0.0)
            slope = own[3] + member(ref, k, 3)
            strength = w * (slope * cubic(w, gd) + cubic(w, gp))
            pulls = [strength * gap for gap in gaps]
            for c in range(3):
                sums[c] = sums[c] + pulls[c]
            for t, (r, s) in enumerate(stress_pairs):
                sums[3 + t] = sums[3 + t] + gaps[r] * pulls[s]
        return tuple(sums)

    sums = offsets_loop(reach, packs, packs_turned, force_step, (zero,) * 9)
    slot = slot_ref[...]
    alive = slot >= 0
    index = jnp.maximum(slot, 0)

    def restored(values, scale):
        moved = jnp.take_along_axis(values, index, axis=1)
        return jnp.where(alive, moved * (scale * p[3]), 0.0)

    for c in range(3):
        force = restored(sums[c], 10.0 / cutoff)
        frc_ref[c] = force
        vel_ref[c] = half_ref[c] + kick_scale * force
    for t in range(6):
        str_ref[t] = restored(sums[3 + t], 5.0 / atom_volume)


def shifted(block, axis, distance):
    count = lax.axis_size(axis)
    route = [(i, (i + distance) % count) for i in range(count)]
    return lax.ppermute(block, axis, route)


def body(position, velocity, force_old, counts, density_coef, pair_coef, embed_coef):
    shape = position.shape
    flat = (3, 8, SLOTS)
    vmem = pl.BlockSpec(memory_space=pltpu.VMEM)
    smem = pl.BlockSpec(memory_space=pltpu.SMEM)
    hbm = pl.BlockSpec(memory_space=pltpu.HBM)
    f32 = jnp.float32
    new, half, pay, slot = pl.pallas_call(
        place_kernel,
        in_specs=[hbm] * 4,
        out_specs=[vmem] * 4,
        out_shape=[jax.ShapeDtypeStruct(flat, f32)] * 3
        + [jax.ShapeDtypeStruct((8, SLOTS), jnp.int32)],
        scratch_shapes=[
            pltpu.VMEM((3,) + flat, f32),
            pltpu.SMEM(counts.shape, jnp.int32),
            pltpu.SemaphoreType.DMA((4,)),
        ],
        compiler_params=pltpu.CompilerParams(vmem_limit_bytes=GRANT),
        name="place",
    )(
        *[
            pltpu.with_memory_space_constraint(source, pltpu.HBM)
            for source in (
                counts,
                position.reshape(flat),
                velocity.reshape(flat),
                force_old.reshape(flat),
            )
        ],
    )
    pay = pay.reshape(shape)
    before = shifted(pay, "gx", 1)
    after = shifted(pay, "gx", -1)
    mid = jnp.concatenate([before, pay, after], axis=1)
    count = lax.axis_size("gy")
    even = lax.axis_index("gy") % 2 == 0
    swap = [(i, i + 1 - 2 * (i % 2)) for i in range(count)]
    mate = lax.ppermute(mid, "gy", swap)
    passed = jnp.where(even, mid[:, :, :2], mid[:, :, 2:])
    route = [(i, (i - 1 + 2 * (i % 2)) % count) for i in range(count)]
    far = lax.ppermute(passed, "gy", route)
    early = pl.pallas_call(
        early_kernel,
        in_specs=[smem] * 3 + [vmem] * 2,
        out_specs=[vmem] * 4,
        out_shape=[jax.ShapeDtypeStruct((r, SLOTS), f32) for r in (16, 16, 8)]
        + [jax.ShapeDtypeStruct(flat, f32)],
        scratch_shapes=[pltpu.VMEM((216, SLOTS), f32), pltpu.VMEM((2, 216, SLOTS), f32)],
        cost_estimate=pl.CostEstimate(flops=12000000, bytes_accessed=60000, transcendentals=0),
        compiler_params=pltpu.CompilerParams(vmem_limit_bytes=GRANT),
        name="early",
    )
    total, coefs, extent, moved = early(density_coef, pair_coef, embed_coef, mid, new)
    rim_scratch = [
        pltpu.VMEM((72, SLOTS), f32),
        pltpu.VMEM((2, 72, SLOTS), f32),
        pltpu.VMEM((2, 3, 8, SLOTS), f32),
    ]
    past_mate = pl.pallas_call(
        mate_kernel,
        in_specs=[vmem] * 4,
        out_specs=[vmem] * 2,
        out_shape=[jax.ShapeDtypeStruct((8, SLOTS), f32)] * 2,
        scratch_shapes=rim_scratch,
        cost_estimate=pl.CostEstimate(flops=5000000, bytes_accessed=60000, transcendentals=0),
        compiler_params=pltpu.CompilerParams(vmem_limit_bytes=GRANT),
        name="past_mate",
    )
    rim, wide = past_mate(mid, mate, coefs, extent)
    vel, frc, stress = pl.pallas_call(
        late_kernel,
        in_specs=[vmem] * 9,
        out_specs=[vmem] * 3,
        out_shape=[
            jax.ShapeDtypeStruct(flat, f32),
            jax.ShapeDtypeStruct(flat, f32),
            jax.ShapeDtypeStruct((6, 8, SLOTS), f32),
        ],
        scratch_shapes=rim_scratch
        + [
            pltpu.VMEM((8, SLOTS), f32),
            pltpu.VMEM((24, SLOTS), f32),
            pltpu.VMEM((288, SLOTS), f32),
            pltpu.VMEM((2, 288, SLOTS), f32),
        ],
        compiler_params=pltpu.CompilerParams(vmem_limit_bytes=GRANT),
        name="late",
    )(mid, mate, far, half, slot, total, rim, coefs, wide)
    return (
        moved.reshape(shape),
        vel.reshape(shape),
        frc.reshape(shape),
        stress.reshape((6,) + shape[1:]),
    )


def solution(mesh):
    grid = P(None, "gx", "gy", None)
    return jax.shard_map(
        body,
        mesh=mesh,
        in_specs=(grid, grid, grid, P("gx", "gy"), P(), P(), P()),
        out_specs=(grid, grid, grid, grid),
        check_vma=False,
    )
```
